128 devices in a mesh: row: 16 (over y, x), col: 8 (over z, core).
Axes of the slice: x: 4, y: 4, z: 4, core: 2. Of those that a mesh axis runs over, the one named last changes fastest.
Arguments:
- features: float32 [32768, 256], P(('row', 'col')), may hold values from -6 to 6
- loader_perm: int32 [32768], P(('row', 'col')), may hold values from 0 to 32767, as said below
- block_values: float32 [16, 8, 256, 4096], P('row', 'col'), may hold values from -0.09375 to 0.09375
- block_row: int32 [16, 8, 256], P('row', 'col'), may hold values from 0 to 63
- block_column: int32 [16, 8, 256], P('row', 'col'), may hold values from 0 to 31
- tile_count: int32 [16, 8], P('row', 'col'), may hold values from 32 to 256, as said below
- weight: float32 [256, 256], replicated, may hold values from -0.375 to 0.375
- bias_vector: float32 [256], replicated, may hold values from -0.5 to 0.5
- cotangent: float32 [32768, 256], P(('row', 'col')), may hold values from -6 to 6
Outputs:
- output: float32 [32768, 256], P(('row', 'col'))
- grad_x: float32 [32768, 256], P(('row', 'col'))
- grad_w: float32 [256, 256], replicated
- grad_b: float32 [256], replicated
The draws below stay inside these ranges and needn't reach their ends.
Inputs may be any that keep to these rules, and one draw needn't show every extreme that they name: `loader_perm`: every grid position appears once; the 256 loader rows of any one device name the same number of positions, 256 divided by the number of devices, in each aligned block of 256 grid positions. `tile_count`: every count is 256 divided by 1, 2, 4 or 8; a block position may appear in several slots of a tile, and such blocks add.
All inputs are finite; a program needn't handle non-finite values.
Results may differ from the reference program's by a relative error of at most 0.0003.
Values sent between devices are 32-bit elements; how exact they have to be, the bound alone decides.
No kernel may reach another device: no remote copies, remote signals or barrier semaphores. Data moves between devices by JAX's collectives and lax.ppermute only.
A program may use at most 128 MiB of HBM per device.

```python
import math
import jax
import jax.numpy as jnp
from jax import lax

F = 256
BS = 64
NODE_DEV = 256
BLK_TILE = 256
NODES = 32768
N_ROW = 16
N_COL = 8


def draw_loader_perm(key, part):
    devices = N_ROW * N_COL
    per_device = NODE_DEV // devices
    key_dest = jax.random.fold_in(key, 11)
    key_source = jax.random.fold_in(key, 12)
    dest_perm = jax.vmap(lambda one_key: jax.random.permutation(one_key, NODE_DEV))(jax.random.split(key_dest, devices)).astype(jnp.int32)
    dest_index = jnp.arange(devices, dtype=jnp.int32)[None, :, None]
    source_index = jnp.arange(devices, dtype=jnp.int32)[:, None, None]
    within = jnp.arange(per_device, dtype=jnp.int32)[None, None, :]
    positions = dest_index * NODE_DEV + dest_perm[dest_index, source_index * per_device + within]
    positions = positions.reshape(devices, NODE_DEV)
    shuffle = jax.vmap(lambda one_key: jax.random.permutation(one_key, NODE_DEV))(jax.random.split(key_source, devices)).astype(jnp.int32)
    positions = jnp.take_along_axis(positions, shuffle, axis=1)
    return positions.reshape(-1).astype(jnp.int32)


def draw_tile_count(key, part):
    tiles = N_ROW * N_COL
    shifts = jax.random.randint(jax.random.fold_in(key, 21), (tiles,), 0, 4).astype(jnp.int32)
    first_tile = jax.random.randint(jax.random.fold_in(key, 22), (), 0, tiles).astype(jnp.int32)
    second_tile = (first_tile + 1 + jax.random.randint(jax.random.fold_in(key, 23), (), 0, tiles - 1).astype(jnp.int32)) % tiles
    shifts = shifts.at[first_tile].set(0).at[second_tile].set(3)
    counts = jnp.right_shift(jnp.full((tiles,), BLK_TILE, jnp.int32), shifts)
    return counts.reshape(N_ROW, N_COL).astype(jnp.int32)


def place_ends(entries, stream_key, smallest, high):
    longest = entries.shape.index(max(entries.shape))
    spots = []
    for shift in (0, 1):
        where = [jax.random.randint(jax.random.fold_in(stream_key, axis), (), 0, length) for axis, length in enumerate(entries.shape)]
        where[longest] = (where[longest] + shift) % entries.shape[longest]
        spots.append(tuple(where))
    return entries.at[spots[0]].set(smallest).at[spots[1]].set(high)


def steps_of(own_key, shape, shards, least, high):
    loudness = 1.0
    for axis_at, shards_of in shards:
        draws = jax.random.uniform(jax.random.fold_in(jax.random.fold_in(own_key, 6), axis_at), (shards_of,), jnp.float32, least / len(shards), high / len(shards))
        loudness = loudness * jnp.repeat(jnp.exp(draws), shape[axis_at] // shards_of).reshape((-1,) + (1,) * (len(shape) - 1 - axis_at))
    return loudness


def centred(own_key, shape, spread, most, pieces=(), held_as=jnp.bfloat16):
    array = jax.random.normal(own_key, shape, jnp.float32) * spread
    if len(pieces) > 0:
        array = steps_of(own_key, shape, pieces, -0.22, 0.18) * array
    return jnp.clip(array, min=-most, max=most).astype(held_as)


def setup_inputs(seed: int = 0) -> dict:
    splits = jax.random.split(jax.random.key(seed), 10)
    features = centred(splits[0], (NODES, F), 1.0, 6.0, ((0, 128),), jnp.float32)
    loader_perm = draw_loader_perm(jax.random.fold_in(splits[9], 71), 0)
    block_values = centred(splits[2], (N_ROW, N_COL, BLK_TILE, BS * BS), (BLK_TILE * BS * BS // NODE_DEV) ** -0.5, 0.09375, ((0, 16), (1, 8)), jnp.float32)
    block_row = place_ends(jax.random.randint(splits[3], (N_ROW, N_COL, BLK_TILE), 0, N_ROW * NODE_DEV // BS), jax.random.fold_in(splits[3], 1), 0, (N_ROW * NODE_DEV // BS) - 1).astype(jnp.int32)
    block_column = place_ends(jax.random.randint(splits[4], (N_ROW, N_COL, BLK_TILE), 0, N_COL * NODE_DEV // BS), jax.random.fold_in(splits[4], 1), 0, (N_COL * NODE_DEV // BS) - 1).astype(jnp.int32)
    tile_count = draw_tile_count(jax.random.fold_in(splits[9], 71), 0)
    weight = centred(splits[6], (F, F), F ** -0.5, 0.375, (), jnp.float32)
    bias_vector = jnp.clip(jax.random.uniform(splits[7], (F,), jnp.float32, -0.5, 0.5), -0.5, 0.5)
    cotangent = centred(splits[8], (NODES, F), 1.0, 6.0, ((0, 128),), jnp.float32)
    return dict(features=features, loader_perm=loader_perm, block_values=block_values, block_row=block_row, block_column=block_column, tile_count=tile_count, weight=weight, bias_vector=bias_vector, cotangent=cotangent)


precise = lax.Precision.HIGHEST

def aggregate(source, block_values, block_row, block_column, tile_count, transpose):
    offsets = jnp.arange(BS, dtype=jnp.int32)
    slots = jnp.arange(BLK_TILE, dtype=jnp.int32)

    def one_tile(accumulated, tile):
        tile_row = tile // N_COL
        tile_col = tile % N_COL
        tile_vals = block_values[tile_row, tile_col].astype(source.dtype).reshape(BLK_TILE, BS, BS)
        alive = (slots < tile_count[tile_row, tile_col]).astype(source.dtype)
        tile_vals = tile_vals * alive[:, None, None]
        row_first = block_row[tile_row, tile_col].astype(jnp.int32) * BS
        out_first = (row_first // NODE_DEV * N_COL + tile_col) * NODE_DEV + row_first % NODE_DEV
        in_first = tile_row * (N_COL * NODE_DEV) + block_column[tile_row, tile_col].astype(jnp.int32) * BS
        out_at = out_first[:, None] + offsets[None, :]
        in_at = in_first[:, None] + offsets[None, :]
        if transpose:
            terms = jnp.einsum('kba,kbf->kaf', tile_vals, source[out_at], precision=precise)
            return (accumulated.at[in_at].add(terms), None)
        terms = jnp.einsum('kab,kbf->kaf', tile_vals, source[in_at], precision=precise)
        return (accumulated.at[out_at].add(terms), None)
    tiles = jnp.arange(N_ROW * N_COL, dtype=jnp.int32)
    accumulated, _ = lax.scan(one_tile, jnp.zeros(source.shape, source.dtype), tiles)
    return accumulated

def reference(features, loader_perm, block_values, block_row, block_column, tile_count, weight, bias_vector, cotangent):
    grid = jnp.zeros(features.shape, features.dtype).at[loader_perm].set(features)
    hidden = aggregate(grid, block_values, block_row, block_column, tile_count, False)
    preact = jnp.dot(hidden, weight, precision=precise) + bias_vector
    squashed = jax.nn.sigmoid(preact)
    output = preact * squashed
    grad_pre = cotangent * squashed * (1.0 + preact * (1.0 - squashed))
    grad_hidden = jnp.dot(grad_pre, weight.T, precision=precise)
    grad_x = aggregate(grad_hidden, block_values, block_row, block_column, tile_count, True)
    norm_scale = 1.0 / math.sqrt(NODES)
    grad_w = jnp.einsum('nf,ng->fg', hidden, grad_pre, precision=precise) * norm_scale
    grad_b = lax.optimization_barrier(jnp.sum(grad_pre, axis=0)) * norm_scale
    return (output, grad_x, grad_w, grad_b)
```

```python
import functools
import math

import jax
import jax.numpy as jnp
from jax import lax
from jax.experimental import pallas as pl
from jax.experimental.pallas import tpu as pltpu
from jax.sharding import PartitionSpec as P

precise = lax.Precision.HIGHEST
F = 256
BS = 64
NODE = 256
SLOTS = 256
STEP = 32
ROWS = 16
COLS = 8
SIDE = 4
LANES = 128
W_ROWS = 40


f32 = jnp.float32
bf16 = jnp.bfloat16


def whole():
    return pl.BlockSpec(memory_space=pltpu.VMEM)


def anywhere():
    return pl.BlockSpec(memory_space=pl.ANY)


def row_hop(dy, dx):
    return [
        (y * SIDE + x, (y + dy) % SIDE * SIDE + (x + dx) % SIDE)
        for y in range(SIDE)
        for x in range(SIDE)
    ]


def col_hop(dz, dc):
    return [
        (z * 2 + c, (z + dz) % SIDE * 2 + (c + dc) % 2) for z in range(SIDE) for c in range(2)
    ]


def pack_kernel(features, perm_row, perm_col, sent):
    owner_row = lax.shift_right_logical(perm_row[...], 8)
    owner_col = lax.shift_right_logical(perm_col[...], 8)
    first = lax.broadcasted_iota(jnp.int32, (NODE, NODE), 0)
    second = lax.broadcasted_iota(jnp.int32, (NODE, NODE), 1)
    earlier = (owner_col == owner_row) & (first < second)
    rank = jnp.sum(earlier.astype(f32), axis=0, keepdims=True).astype(jnp.int32)
    chosen = (first == owner_row * 2 + rank).astype(f32)
    sent[:, :F] = jnp.dot(chosen, features[...], precision=precise, preferred_element_type=f32)
    place = (perm_row[...] & (NODE - 1)).astype(f32)
    place = jnp.sum(chosen * place, axis=1, keepdims=True)
    sent[:, F:] = jnp.broadcast_to(place, (NODE, LANES))


def pack(features, perm):
    return pl.pallas_call(
        pack_kernel,
        out_shape=jax.ShapeDtypeStruct((NODE, F + LANES), f32),
        in_specs=[whole()] * 3,
        out_specs=whole(),
        name="pack",
    )(features, perm.reshape(1, NODE), perm.reshape(NODE, 1))


def place_kernel(got, own):
    place = got[:, F:].astype(jnp.int32)
    place = jnp.concatenate([place, place], axis=1)
    second = lax.broadcasted_iota(jnp.int32, (NODE, NODE), 1)
    chosen = (place == second).astype(f32).T
    own[...] = jnp.dot(chosen, got[:, :F], precision=precise, preferred_element_type=f32)


def place(got):
    return pl.pallas_call(
        place_kernel,
        out_shape=jax.ShapeDtypeStruct((NODE, F), f32),
        in_specs=[whole()],
        out_specs=whole(),
        name="place",
    )(got)


def prepare_kernel(vals, forward, backward, lines):
    for group in range(STEP // 8):
        for tile in range(BS * BS // LANES):
            lines[pl.ds(group * 8 * 32 + tile, 8, stride=32), :] = vals[
                pl.ds(group * 8, 8), pl.ds(tile * LANES, LANES)
            ]
    left = lax.broadcasted_iota(jnp.int32, (32, LANES), 1) < BS

    def one(slot, carry):
        pair = lines[pl.ds(pl.multiple_of(slot * 32, 32), 32), :]
        turned = pltpu.roll(pair, BS, 1)
        block = jnp.concatenate(
            [jnp.where(left, pair, turned), jnp.where(left, turned, pair)], axis=0
        )
        high = block.astype(bf16)
        forward[slot, :, :LANES] = high
        forward[slot, :, LANES:] = (block - high.astype(f32)).astype(bf16)
        flipped = jnp.concatenate([block, block], axis=0).T[:BS]
        high = flipped.astype(bf16)
        backward[slot, :, :LANES] = high
        backward[slot, :, LANES:] = (flipped - high.astype(f32)).astype(bf16)
        return carry

    lax.fori_loop(0, STEP, one, 0, unroll=4)


def prepare(vals, count):
    steps = SLOTS // STEP

    def at(step, count):
        return jnp.minimum(step, count[0] // STEP - 1)

    return pl.pallas_call(
        prepare_kernel_skip,
        out_shape=[jax.ShapeDtypeStruct((SLOTS, BS, F), bf16)] * 2,
        grid_spec=pltpu.PrefetchScalarGridSpec(
            num_scalar_prefetch=1,
            grid=(steps,),
            in_specs=[pl.BlockSpec((STEP, BS * BS), lambda s, n: (at(s, n), 0))],
            out_specs=[pl.BlockSpec((STEP, BS, F), lambda s, n: (at(s, n), 0, 0))] * 2,
            scratch_shapes=[pltpu.VMEM((STEP * 32, LANES), f32)],
        ),
        cost_estimate=pl.CostEstimate(flops=10**8, bytes_accessed=20 << 20, transcendentals=0),
        name="prepare",
    )(count, vals)


def prepare_kernel_skip(count, vals, forward, backward, lines):
    @pl.when(pl.program_id(0) * STEP < count[0])
    def _():
        prepare_kernel(vals, forward, backward, lines)


def aggregate_kernel(n_src, n_dst, *refs):
    source_at, target_at, count = refs[:3]
    blocks = refs[3]
    sources = refs[4 : 4 + n_src]
    targets = refs[4 + n_src : 4 + n_src + n_dst]
    held, split, total, in_sems, out_sems = refs[4 + n_src + n_dst :]
    step = pl.program_id(0)
    in_rows = sources[0].shape[0]
    out_rows = targets[0].shape[0]

    def load(n):
        return pltpu.make_async_copy(
            sources[n], held.at[pl.ds(n * in_rows, in_rows)], in_sems.at[n]
        )

    def keep(n):
        return pltpu.make_async_copy(
            total.at[pl.ds(n * out_rows, out_rows)], targets[n], out_sems.at[n]
        )

    @pl.when(step == 0)
    def _():
        for n in range(n_src):
            load(n).start()
        total[...] = jnp.zeros_like(total)
        per = in_rows // BS
        for n in range(n_src):
            load(n).wait()

            def one(k, carry):
                at = n * per + k
                rows = held[pl.ds(pl.multiple_of(at * BS, BS), BS), :]
                high = rows.astype(bf16)
                low = (rows - high.astype(f32)).astype(bf16)
                split[at, 0:BS, :] = high
                split[at, BS : 2 * BS, :] = low
                split[at, 2 * BS : 3 * BS, :] = high
                split[at, 3 * BS :, :] = low
                return carry

            lax.fori_loop(0, per, one, 0, unroll=2)

    @pl.when(step * STEP < count[0])
    def _():
        def eight(turn, carry):
            for k in range(8):
                slot = turn * 8 + k
                at = step * STEP + slot
                term = jnp.dot(
                    blocks[slot], split[source_at[at]], preferred_element_type=f32
                )
                into = pl.ds(pl.multiple_of(target_at[at] * BS, BS), BS)
                total[into, :] += term
            return carry

        lax.fori_loop(0, STEP // 8, eight, 0)

    @pl.when(step == pl.num_programs(0) - 1)
    def _():
        for n in range(n_dst):
            keep(n).start()
        for n in range(n_dst):
            keep(n).wait()


def aggregate(blocks, sources, source_at, target_at, count, n_dst, out_rows, name):
    n_src = len(sources)
    total_in = sum(s.shape[0] for s in sources)
    steps = SLOTS // STEP
    return pl.pallas_call(
        functools.partial(aggregate_kernel, n_src, n_dst),
        out_shape=[jax.ShapeDtypeStruct((out_rows // n_dst, F), f32)] * n_dst,
        grid_spec=pltpu.PrefetchScalarGridSpec(
            num_scalar_prefetch=3,
            grid=(steps,),
            in_specs=[
                pl.BlockSpec(
                    (STEP, BS, F),
                    lambda s, a, b, n: (jnp.minimum(s, n[0] // STEP - 1), 0, 0),
                )
            ]
            + [anywhere()] * n_src,
            out_specs=[anywhere()] * n_dst,
            scratch_shapes=[
                pltpu.VMEM((total_in, F), f32),
                pltpu.VMEM((total_in // BS, 4 * BS, F), bf16),
                pltpu.VMEM((out_rows, F), f32),
                pltpu.SemaphoreType.DMA((n_src,)),
                pltpu.SemaphoreType.DMA((n_dst,)),
            ],
        ),
        cost_estimate=pl.CostEstimate(
            flops=2 * SLOTS * BS * F * F, bytes_accessed=16 << 20, transcendentals=0
        ),
        name=name,
    )(source_at, target_at, count, blocks, *sources)


def middle_kernel(*refs):
    parts, (weight, bias, cotangent) = refs[:8], refs[8:11]
    output, grad_a, grad_b, sums, hidden, turned, strip = refs[11:]
    half = NODE // 2
    hidden[:half] = parts[0][...] + parts[1][...] + parts[2][...] + parts[3][...]
    hidden[half:] = parts[4][...] + parts[5][...] + parts[6][...] + parts[7][...]
    for side in range(2):
        lanes = slice(side * LANES, (side + 1) * LANES)
        strip[side * NODE : (side + 1) * NODE] = cotangent[:, lanes]
        for q in range(NODE // BS):
            for odd in range(2):
                turned[pl.ds(q * BS + odd * 32, 32), lanes] = strip[
                    pl.ds(side * NODE + q * BS + odd, 32, stride=2), :
                ]
    rows = hidden[...]
    preact = jnp.dot(rows, weight[...], precision=precise, preferred_element_type=f32)
    preact = preact + bias[...]
    squashed = 1.0 / (1.0 + jnp.exp(-preact))
    grad_pre = turned[...] * squashed * (1.0 + preact * (1.0 - squashed))
    turned[...] = preact * squashed
    grad = lax.dot_general(
        grad_pre, weight[...], (((1,), (1,)), ((), ())), precision=precise,
        preferred_element_type=f32,
    )
    grad_a[...] = grad[:half]
    grad_b[...] = grad[half:]
    for side in range(2):
        lanes = slice(side * LANES, (side + 1) * LANES)
        for q in range(NODE // BS):
            for odd in range(2):
                strip[pl.ds(side * NODE + q * BS + odd, 32, stride=2), :] = turned[
                    pl.ds(q * BS + odd * 32, 32), lanes
                ]
        output[:, lanes] = strip[side * NODE : (side + 1) * NODE]
    local_w = jnp.dot(rows.T, grad_pre, precision=precise, preferred_element_type=f32)
    local_b = jnp.sum(grad_pre, axis=0, keepdims=True)
    for n in range(COLS):
        sums[n, 0:32, :] = local_w[n * 32 : (n + 1) * 32]
        sums[n, 32:, :] = jnp.broadcast_to(local_b, (W_ROWS - 32, F))


def middle(parts, weight, bias, cotangent):
    return pl.pallas_call(
        middle_kernel,
        out_shape=[
            jax.ShapeDtypeStruct((NODE, F), f32),
            jax.ShapeDtypeStruct((NODE // 2, F), f32),
            jax.ShapeDtypeStruct((NODE // 2, F), f32),
            jax.ShapeDtypeStruct((COLS, W_ROWS, F), f32),
        ],
        in_specs=[whole()] * 11,
        out_specs=[whole()] * 4,
        scratch_shapes=[pltpu.VMEM((NODE, F), f32)] * 2 + [pltpu.VMEM((2 * NODE, LANES), f32)],
        name="middle",
    )(*parts, weight, bias.reshape(1, F), cotangent)


def on_device(
    features,
    loader_perm,
    block_values,
    block_row,
    block_column,
    tile_count,
    weight,
    bias_vector,
    cotangent,
):
    row = lax.axis_index("row")
    col = lax.axis_index("col")
    my_y, my_x = row // SIDE, row % SIDE
    my_z, my_c = col // 2, col % 2
    count = tile_count.reshape(1)
    tile_rows = block_row.reshape(SLOTS)
    tile_columns = block_column.reshape(SLOTS)

    r_dev, r_q = tile_rows >> 2, tile_rows & 3
    r_y, r_x = r_dev >> 2, r_dev & 3
    c_dev, c_q = tile_columns >> 2, tile_columns & 3
    c_z, c_c = c_dev >> 1, c_dev & 1
    out_d, out_e = (r_x - my_x) & 3, (r_y - my_y) & 3
    in_d, in_e = (my_x - r_x) & 3, (my_y - r_y) & 3

    def row_slot(d, e):
        first = d * 8 + e * 2 + (r_q & 1)
        second = 32 + e * 8 + d * 2 + (r_q & 1)
        return jnp.where(r_q < 2, first, second)

    fwd_to = row_slot(out_d, out_e)
    bwd_from = row_slot(in_d, in_e)
    other = c_c ^ my_c
    fwd_from = (((my_z - c_z) & 3) * 2 + other) * 4 + c_q
    bwd_to = (other * 4 + ((c_z - my_z) & 3)) * 4 + c_q

    sent = pack(features, loader_perm).reshape(ROWS * COLS, 2, F + LANES)
    got = lax.all_to_all(sent, ("row", "col"), split_axis=0, concat_axis=0, tiled=True)
    fwd_blocks, bwd_blocks = prepare(block_values.reshape(SLOTS, BS * BS), count)
    own = place(got.reshape(NODE, F + LANES))
    panel = [own] + [lax.ppermute(own, "col", col_hop(f, 0)) for f in (1, 2, 3)]
    sources = []
    for part in panel:
        sources += [part, lax.ppermute(part, "col", col_hop(0, 1))]

    half = aggregate(
        fwd_blocks, sources, fwd_from, fwd_to, count, 8, ROWS * NODE, "aggregate"
    )
    got_a = [lax.ppermute(half[d], "row", row_hop(0, d)) for d in (1, 2, 3)]
    got_b = [lax.ppermute(half[4 + e], "row", row_hop(e, 0)) for e in (1, 2, 3)]
    n = NODE // 2

    def partial(own_part, got, k):
        cut = slice(k * n, (k + 1) * n)
        return own_part[cut] + got[0][cut] + got[1][cut] + got[2][cut]

    sum_a = [partial(half[0], got_a, k) for k in range(SIDE)]
    sum_b = [partial(half[4], got_b, k) for k in range(SIDE)]
    parts = [sum_a[0]] + [lax.ppermute(sum_a[e], "row", row_hop(e, 0)) for e in (1, 2, 3)]
    parts += [sum_b[0]] + [lax.ppermute(sum_b[d], "row", row_hop(0, d)) for d in (1, 2, 3)]

    output, grad_a, grad_b, sums = middle(parts, weight, bias_vector, cotangent)

    near_a = [grad_a] + [lax.ppermute(grad_a, "row", row_hop(e, 0)) for e in (1, 2, 3)]
    near_b = [grad_b] + [lax.ppermute(grad_b, "row", row_hop(0, d)) for d in (1, 2, 3)]
    near_a = jnp.concatenate(near_a, axis=0)
    near_b = jnp.concatenate(near_b, axis=0)
    column = [near_a] + [lax.ppermute(near_a, "row", row_hop(0, d)) for d in (1, 2, 3)]
    column += [near_b] + [lax.ppermute(near_b, "row", row_hop(e, 0)) for e in (1, 2, 3)]

    sums = lax.all_to_all(sums, "col", split_axis=0, concat_axis=0, tiled=True)
    sums = jnp.sum(sums, axis=0)
    sums = jnp.broadcast_to(sums[None], (ROWS, W_ROWS, F))
    sums = lax.all_to_all(sums, "row", split_axis=0, concat_axis=0, tiled=True)
    norm_scale = 1.0 / math.sqrt(NODE * ROWS * COLS)
    sums = jnp.sum(sums, axis=0) * norm_scale
    sums = jnp.broadcast_to(sums[None], (COLS, W_ROWS, F))
    sums = lax.all_to_all(sums, "col", split_axis=0, concat_axis=0, tiled=True)
    grad_w = sums[:, :32].reshape(F, F)
    grad_bias = sums[0, 32]

    keep, give = aggregate(
        bwd_blocks, column, bwd_from, bwd_to, count, 2, COLS * NODE, "aggregate_back"
    )
    taken = lax.ppermute(give, "col", col_hop(0, 1))
    sums_x = [
        keep[k * NODE : (k + 1) * NODE] + taken[k * NODE : (k + 1) * NODE] for k in range(SIDE)
    ]
    got_x = [lax.ppermute(sums_x[f], "col", col_hop(f, 0)) for f in (1, 2, 3)]
    grad_x = sums_x[0] + got_x[0] + got_x[1] + got_x[2]
    return (output, grad_x, grad_w, grad_bias)


def solution(mesh):
    in_specs = (
        P(("row", "col"), None),
        P(("row", "col")),
        P("row", "col", None, None),
        P("row", "col", None),
        P("row", "col", None),
        P("row", "col"),
        P(),
        P(),
        P(("row", "col"), None),
    )
    out_specs = (P(("row", "col"), None), P(("row", "col"), None), P(), P())
    return jax.shard_map(
        on_device, mesh=mesh, in_specs=in_specs, out_specs=out_specs, check_vma=False
    )
```

```python
import functools
import math

import jax
import jax.numpy as jnp
from jax import lax
from jax.experimental import pallas as pl
from jax.experimental.pallas import tpu as pltpu
from jax.sharding import PartitionSpec as P

precise = lax.Precision.HIGHEST
F = 256
BS = 64
NODE = 256
SLOTS = 256
STEP = 32
DEPTH = 192
ROWS = 16
COLS = 8
SIDE = 4
LANES = 128
W_ROWS = 40


f32 = jnp.float32
bf16 = jnp.bfloat16


def whole():
    return pl.BlockSpec(memory_space=pltpu.VMEM)


def anywhere():
    return pl.BlockSpec(memory_space=pl.ANY)


def row_hop(dy, dx):
    return [
        (y * SIDE + x, (y + dy) % SIDE * SIDE + (x + dx) % SIDE)
        for y in range(SIDE)
        for x in range(SIDE)
    ]


def col_hop(dz, dc):
    return [
        (z * 2 + c, (z + dz) % SIDE * 2 + (c + dc) % 2) for z in range(SIDE) for c in range(2)
    ]


def pack_kernel(features, perm_row, sent):
    owner_row = jnp.broadcast_to(lax.shift_right_logical(perm_row[...], 8), (NODE, NODE))
    owner_col = owner_row.astype(f32).T.astype(jnp.int32)
    first = lax.broadcasted_iota(jnp.int32, (NODE, NODE), 0)
    second = lax.broadcasted_iota(jnp.int32, (NODE, NODE), 1)
    earlier = (owner_col == owner_row) & (first < second)
    rank = jnp.sum(earlier.astype(f32), axis=0, keepdims=True).astype(jnp.int32)
    chosen = (first == owner_row * 2 + rank).astype(f32)
    sent[:, :F] = jnp.dot(chosen, features[...], precision=precise, preferred_element_type=f32)
    place = (perm_row[...] & (NODE - 1)).astype(f32)
    place = jnp.sum(chosen * place, axis=1, keepdims=True)
    sent[:, F:] = jnp.broadcast_to(place, (NODE, LANES))


def pack(features, perm):
    return pl.pallas_call(
        pack_kernel,
        out_shape=jax.ShapeDtypeStruct((NODE, F + LANES), f32),
        in_specs=[whole()] * 2,
        out_specs=whole(),
        name="pack",
    )(features, perm.reshape(1, NODE))


def place_kernel(got, own):
    place = got[:, F:].astype(jnp.int32)
    place = jnp.concatenate([place, place], axis=1)
    second = lax.broadcasted_iota(jnp.int32, (NODE, NODE), 1)
    chosen = (place == second).astype(f32).T
    own[...] = jnp.dot(chosen, got[:, :F], precision=precise, preferred_element_type=f32)


def place(got):
    return pl.pallas_call(
        place_kernel,
        out_shape=jax.ShapeDtypeStruct((NODE, F), f32),
        in_specs=[whole()],
        out_specs=whole(),
        name="place",
    )(got)


def prepare_kernel(flip, count, vals, blocks, lines):
    @pl.when(pl.program_id(0) * STEP < count[0])
    def _():
        for group in range(STEP // 8):
            for tile in range(BS * BS // LANES):
                lines[pl.ds(group * 8 * 32 + tile, 8, stride=32), :] = vals[
                    pl.ds(group * 8, 8), pl.ds(tile * LANES, LANES)
                ]
        left = lax.broadcasted_iota(jnp.int32, (32, LANES), 1) < BS

        def one(slot, carry):
            pair = lines[pl.ds(pl.multiple_of(slot * 32, 32), 32), :]
            turned = pltpu.roll(pair, BS, 1)
            block = jnp.concatenate(
                [jnp.where(left, pair, turned), jnp.where(left, turned, pair)], axis=0
            )
            if flip:
                block = jnp.concatenate([block, block], axis=0).T[:BS]
            high = block.astype(bf16)
            blocks[slot, :, :LANES] = high
            blocks[slot, :, LANES:] = (block - high.astype(f32)).astype(bf16)
            return carry

        lax.fori_loop(0, STEP, one, 0, unroll=8)


def prepare(vals, count, flip):
    def at(step, count):
        return jnp.minimum(step, count[0] // STEP - 1)

    return pl.pallas_call(
        functools.partial(prepare_kernel, flip),
        out_shape=jax.ShapeDtypeStruct((SLOTS, BS, F), bf16),
        grid_spec=pltpu.PrefetchScalarGridSpec(
            num_scalar_prefetch=1,
            grid=(SLOTS // STEP,),
            in_specs=[pl.BlockSpec((STEP, BS * BS), lambda s, n: (at(s, n), 0))],
            out_specs=pl.BlockSpec((STEP, BS, F), lambda s, n: (at(s, n), 0, 0)),
            scratch_shapes=[pltpu.VMEM((STEP * 32, LANES), f32)],
        ),
        cost_estimate=pl.CostEstimate(flops=10**8, bytes_accessed=12 << 20, transcendentals=0),
        name="prepare_back" if flip else "prepare",
    )(count, vals)


def aggregate_kernel(n_src, n_dst, *refs):
    source_at, target_at, count = refs[:3]
    blocks = refs[3]
    sources = refs[4 : 4 + n_src]
    targets = refs[4 + n_src : 4 + n_src + n_dst]
    held, split, total, in_sems, out_sems = refs[4 + n_src + n_dst :]
    step = pl.program_id(0)
    in_rows = sources[0].shape[0]
    out_rows = targets[0].shape[0]

    def load(n):
        return pltpu.make_async_copy(
            sources[n], held.at[pl.ds(n * in_rows, in_rows)], in_sems.at[n]
        )

    def keep(n):
        return pltpu.make_async_copy(
            total.at[pl.ds(n * out_rows, out_rows)], targets[n], out_sems.at[n]
        )

    @pl.when(step == 0)
    def _():
        for n in range(n_src):
            load(n).start()
        total[...] = jnp.zeros_like(total)
        per = in_rows // BS
        for n in range(n_src):
            load(n).wait()

            def one(k, carry):
                at = n * per + k
                rows = held[pl.ds(pl.multiple_of(at * BS, BS), BS), :]
                high = rows.astype(bf16)
                low = (rows - high.astype(f32)).astype(bf16)
                split[at, 0:BS, :] = high
                split[at, BS : 2 * BS, :] = low
                split[at, 2 * BS :, :] = high
                return carry

            lax.fori_loop(0, per, one, 0, unroll=2)

    @pl.when(step * STEP < count[0])
    def _():
        for slot in range(STEP):
            at = step * STEP + slot
            term = jnp.dot(
                blocks[slot][:, :DEPTH], split[source_at[at]], preferred_element_type=f32
            )
            into = pl.ds(pl.multiple_of(target_at[at] * BS, BS), BS)
            total[into, :] += term

    @pl.when(step == pl.num_programs(0) - 1)
    def _():
        for n in range(n_dst):
            keep(n).start()
        for n in range(n_dst):
            keep(n).wait()


def aggregate(blocks, sources, source_at, target_at, count, n_dst, out_rows):
    n_src = len(sources)
    total_in = sum(s.shape[0] for s in sources)
    steps = SLOTS // STEP
    return pl.pallas_call(
        functools.partial(aggregate_kernel, n_src, n_dst),
        out_shape=[jax.ShapeDtypeStruct((out_rows // n_dst, F), f32)] * n_dst,
        grid_spec=pltpu.PrefetchScalarGridSpec(
            num_scalar_prefetch=3,
            grid=(steps,),
            in_specs=[
                pl.BlockSpec(
                    (STEP, BS, F),
                    lambda s, a, b, n: (jnp.minimum(s, n[0] // STEP - 1), 0, 0),
                )
            ]
            + [anywhere()] * n_src,
            out_specs=[anywhere()] * n_dst,
            scratch_shapes=[
                pltpu.VMEM((total_in, F), f32),
                pltpu.VMEM((total_in // BS, DEPTH, F), bf16),
                pltpu.VMEM((out_rows, F), f32),
                pltpu.SemaphoreType.DMA((n_src,)),
                pltpu.SemaphoreType.DMA((n_dst,)),
            ],
        ),
        cost_estimate=pl.CostEstimate(
            flops=2 * SLOTS * BS * F * F, bytes_accessed=16 << 20, transcendentals=0
        ),
    )(source_at, target_at, count, blocks, *sources)


def middle_kernel(*refs):
    parts, (weight, bias, cotangent) = refs[:8], refs[8:11]
    output, grad_a, grad_b, sums, hidden, turned, strip = refs[11:]
    half = NODE // 2
    hidden[:half] = parts[0][...] + parts[1][...] + parts[2][...] + parts[3][...]
    hidden[half:] = parts[4][...] + parts[5][...] + parts[6][...] + parts[7][...]
    for side in range(2):
        lanes = slice(side * LANES, (side + 1) * LANES)
        strip[side * NODE : (side + 1) * NODE] = cotangent[:, lanes]
        for q in range(NODE // BS):
            for odd in range(2):
                turned[pl.ds(q * BS + odd * 32, 32), lanes] = strip[
                    pl.ds(side * NODE + q * BS + odd, 32, stride=2), :
                ]
    rows = hidden[...]
    preact = jnp.dot(rows, weight[...], precision=precise, preferred_element_type=f32)
    preact = preact + bias[...]
    squashed = 1.0 / (1.0 + jnp.exp(-preact))
    grad_pre = turned[...] * squashed * (1.0 + preact * (1.0 - squashed))
    turned[...] = preact * squashed
    grad = lax.dot_general(
        grad_pre, weight[...], (((1,), (1,)), ((), ())), precision=precise,
        preferred_element_type=f32,
    )
    grad_a[...] = grad[:half]
    grad_b[...] = grad[half:]
    for side in range(2):
        lanes = slice(side * LANES, (side + 1) * LANES)
        for q in range(NODE // BS):
            for odd in range(2):
                strip[pl.ds(side * NODE + q * BS + odd, 32, stride=2), :] = turned[
                    pl.ds(q * BS + odd * 32, 32), lanes
                ]
        output[:, lanes] = strip[side * NODE : (side + 1) * NODE]
    local_w = jnp.dot(rows.T, grad_pre, precision=precise, preferred_element_type=f32)
    local_b = jnp.sum(grad_pre, axis=0, keepdims=True)
    for n in range(COLS):
        sums[n, 0:32, :] = local_w[n * 32 : (n + 1) * 32]
        sums[n, 32:, :] = jnp.broadcast_to(local_b, (W_ROWS - 32, F))


def middle(parts, weight, bias, cotangent):
    return pl.pallas_call(
        middle_kernel,
        out_shape=[
            jax.ShapeDtypeStruct((NODE, F), f32),
            jax.ShapeDtypeStruct((NODE // 2, F), f32),
            jax.ShapeDtypeStruct((NODE // 2, F), f32),
            jax.ShapeDtypeStruct((COLS, W_ROWS, F), f32),
        ],
        in_specs=[whole()] * 11,
        out_specs=[whole()] * 4,
        scratch_shapes=[pltpu.VMEM((NODE, F), f32)] * 2 + [pltpu.VMEM((2 * NODE, LANES), f32)],
        name="middle",
    )(*parts, weight, bias.reshape(1, F), cotangent)


def on_device(
    features,
    loader_perm,
    block_values,
    block_row,
    block_column,
    tile_count,
    weight,
    bias_vector,
    cotangent,
):
    row = lax.axis_index("row")
    col = lax.axis_index("col")
    my_y, my_x = row // SIDE, row % SIDE
    my_z, my_c = col // 2, col % 2
    count = tile_count.reshape(1)
    tile_rows = block_row.reshape(SLOTS)
    tile_columns = block_column.reshape(SLOTS)

    r_dev, r_q = tile_rows >> 2, tile_rows & 3
    r_y, r_x = r_dev >> 2, r_dev & 3
    c_dev, c_q = tile_columns >> 2, tile_columns & 3
    c_z, c_c = c_dev >> 1, c_dev & 1
    out_d, out_e = (r_x - my_x) & 3, (r_y - my_y) & 3
    in_d, in_e = (my_x - r_x) & 3, (my_y - r_y) & 3

    def row_slot(d, e):
        first = d * 8 + e * 2 + (r_q & 1)
        second = 32 + e * 8 + d * 2 + (r_q & 1)
        return jnp.where(r_q < 2, first, second)

    fwd_to = row_slot(out_d, out_e)
    bwd_from = row_slot(in_d, in_e)
    other = c_c ^ my_c
    fwd_from = (((my_z - c_z) & 3) * 2 + other) * 4 + c_q
    bwd_to = (other * 4 + ((c_z - my_z) & 3)) * 4 + c_q

    sent = pack(features, loader_perm).reshape(ROWS * COLS, 2, F + LANES)
    got = lax.all_to_all(sent, ("row", "col"), split_axis=0, concat_axis=0, tiled=True)
    vals = block_values.reshape(SLOTS, BS * BS)
    fwd_blocks = prepare(vals, count, False)
    got, fwd_blocks = lax.optimization_barrier((got, fwd_blocks))
    own = place(got.reshape(NODE, F + LANES))
    panel = [own] + [lax.ppermute(own, "col", col_hop(f, 0)) for f in (1, 2, 3)]
    sources = []
    for part in panel:
        sources += [part, lax.ppermute(part, "col", col_hop(0, 1))]

    half = list(aggregate(
        fwd_blocks, sources, fwd_from, fwd_to, count, 8, ROWS * NODE)
    )
    got_a = [lax.ppermute(half[d], "row", row_hop(0, d)) for d in (1, 2, 3)]
    got_b = [lax.ppermute(half[4 + e], "row", row_hop(e, 0)) for e in (1, 2, 3)]
    n = NODE // 2
    back_count, half[0] = lax.optimization_barrier((count, half[0]))
    bwd_blocks = prepare(vals, back_count, True)
    got_a[0], bwd_blocks = lax.optimization_barrier((got_a[0], bwd_blocks))

    def partial(own_part, got, k):
        cut = slice(k * n, (k + 1) * n)
        return own_part[cut] + got[0][cut] + got[1][cut] + got[2][cut]

    sum_a = [partial(half[0], got_a, k) for k in range(SIDE)]
    sum_b = [partial(half[4], got_b, k) for k in range(SIDE)]
    parts = [sum_a[0]] + [lax.ppermute(sum_a[e], "row", row_hop(e, 0)) for e in (1, 2, 3)]
    parts += [sum_b[0]] + [lax.ppermute(sum_b[d], "row", row_hop(0, d)) for d in (1, 2, 3)]

    output, grad_a, grad_b, sums = middle(parts, weight, bias_vector, cotangent)

    near_a = [grad_a] + [lax.ppermute(grad_a, "row", row_hop(e, 0)) for e in (1, 2, 3)]
    near_b = [grad_b] + [lax.ppermute(grad_b, "row", row_hop(0, d)) for d in (1, 2, 3)]
    near_a = jnp.concatenate(near_a, axis=0)
    near_b = jnp.concatenate(near_b, axis=0)
    column = [near_a] + [lax.ppermute(near_a, "row", row_hop(0, d)) for d in (1, 2, 3)]
    column += [near_b] + [lax.ppermute(near_b, "row", row_hop(e, 0)) for e in (1, 2, 3)]

    sums = lax.all_to_all(sums, "col", split_axis=0, concat_axis=0, tiled=True)
    sums = jnp.sum(sums, axis=0)
    sums = jnp.broadcast_to(sums[None], (ROWS, W_ROWS, F))
    bwd_from, sums = lax.optimization_barrier((bwd_from, sums))
    sums = lax.all_to_all(sums, "row", split_axis=0, concat_axis=0, tiled=True)
    keep, give = aggregate(bwd_blocks, column, bwd_from, bwd_to, count, 2, COLS * NODE)
    taken = lax.ppermute(give, "col", col_hop(0, 1))
    keep, sums = lax.optimization_barrier((keep, sums))
    sums_x = [
        keep[k * NODE : (k + 1) * NODE] + taken[k * NODE : (k + 1) * NODE] for k in range(SIDE)
    ]
    got_x = [lax.ppermute(sums_x[f], "col", col_hop(f, 0)) for f in (1, 2, 3)]
    norm_scale = 1.0 / math.sqrt(NODE * ROWS * COLS)
    sums = jnp.sum(sums, axis=0) * norm_scale
    sums = jnp.broadcast_to(sums[None], (COLS, W_ROWS, F))
    sums = lax.all_to_all(sums, "col", split_axis=0, concat_axis=0, tiled=True)
    grad_w = sums[:, :32].reshape(F, F)
    grad_bias = sums[0, 32]
    grad_x = sums_x[0] + got_x[0] + got_x[1] + got_x[2]
    return (output, grad_x, grad_w, grad_bias)


def solution(mesh):
    in_specs = (
        P(("row", "col"), None),
        P(("row", "col")),
        P("row", "col", None, None),
        P("row", "col", None),
        P("row", "col", None),
        P("row", "col"),
        P(),
        P(),
        P(("row", "col"), None),
    )
    out_specs = (P(("row", "col"), None), P(("row", "col"), None), P(), P())

    return jax.shard_map(
        on_device, mesh=mesh, in_specs=in_specs, out_specs=out_specs, check_vma=False
    )
```

```python
import functools
import math

import jax
import jax.numpy as jnp
from jax import lax
from jax.experimental import pallas as pl
from jax.experimental.pallas import tpu as pltpu
from jax.sharding import PartitionSpec as P

precise = lax.Precision.HIGHEST
F = 256
BS = 64
NODE = 256
SLOTS = 256
STEP = 32
DEPTH = 192
ROWS = 16
COLS = 8
SIDE = 4
LANES = 128
W_ROWS = 40


f32 = jnp.float32
bf16 = jnp.bfloat16


def room(mib):
    return pltpu.CompilerParams(vmem_limit_bytes=mib << 20)


def whole():
    return pl.BlockSpec(memory_space=pltpu.VMEM)


def anywhere():
    return pl.BlockSpec(memory_space=pl.ANY)


def row_hop(dy, dx):
    return [
        (y * SIDE + x, (y + dy) % SIDE * SIDE + (x + dx) % SIDE)
        for y in range(SIDE)
        for x in range(SIDE)
    ]


def col_hop(dz, dc):
    return [
        (z * 2 + c, (z + dz) % SIDE * 2 + (c + dc) % 2) for z in range(SIDE) for c in range(2)
    ]


def pack_kernel(features, perm_row, sent):
    owner_row = jnp.broadcast_to(lax.shift_right_logical(perm_row[...], 8), (NODE, NODE))
    owner_col = owner_row.astype(f32).T.astype(jnp.int32)
    first = lax.broadcasted_iota(jnp.int32, (NODE, NODE), 0)
    second = lax.broadcasted_iota(jnp.int32, (NODE, NODE), 1)
    earlier = (owner_col == owner_row) & (first < second)
    rank = jnp.sum(earlier.astype(f32), axis=0, keepdims=True).astype(jnp.int32)
    slot = owner_row[:1] * 2 + rank
    spot = (perm_row[...] & (NODE - 1)).astype(f32)
    rows = lax.broadcasted_iota(jnp.int32, (NODE // 2, NODE), 0)
    for n in range(2):
        chosen = (rows * 2 + n == slot).astype(f32)
        sent[:, n, :F] = jnp.dot(
            chosen, features[...], precision=precise, preferred_element_type=f32
        )
        spots = jnp.sum(chosen * spot, axis=1, keepdims=True)
        sent[:, n, F:] = jnp.broadcast_to(spots, (NODE // 2, LANES))


def pack(features, perm):
    return pl.pallas_call(
        pack_kernel,
        out_shape=jax.ShapeDtypeStruct((NODE // 2, 2, F + LANES), f32),
        in_specs=[whole()] * 2,
        out_specs=whole(),
        compiler_params=room(8),
        name="pack",
    )(features, perm.reshape(1, NODE))


def place_kernel(got, own):
    second = lax.broadcasted_iota(jnp.int32, (NODE // 2, NODE), 1)
    chosen, rows = [], []
    for n in range(2):
        spot = got[:, n, F:].astype(jnp.int32)
        chosen.append((jnp.concatenate([spot, spot], axis=1) == second).astype(f32))
        rows.append(got[:, n, :F])
    chosen = jnp.concatenate(chosen, axis=0).T
    rows = jnp.concatenate(rows, axis=0)
    own[...] = jnp.dot(chosen, rows, precision=precise, preferred_element_type=f32)


def place(got):
    return pl.pallas_call(
        place_kernel,
        out_shape=jax.ShapeDtypeStruct((NODE, F), f32),
        in_specs=[whole()],
        out_specs=whole(),
        compiler_params=room(8),
        name="place",
    )(got)


def prepare_kernel(flip, count, vals, blocks, lines):
    @pl.when(pl.program_id(0) * STEP < count[0])
    def _():
        for group in range(STEP // 8):
            for tile in range(BS * BS // LANES):
                lines[pl.ds(group * 8 * 32 + tile, 8, stride=32), :] = vals[
                    pl.ds(group * 8, 8), pl.ds(tile * LANES, LANES)
                ]
        left = lax.broadcasted_iota(jnp.int32, (32, LANES), 1) < BS

        def one(slot, carry):
            pair = lines[pl.ds(pl.multiple_of(slot * 32, 32), 32), :]
            turned = pltpu.roll(pair, BS, 1)
            block = jnp.concatenate(
                [jnp.where(left, pair, turned), jnp.where(left, turned, pair)], axis=0
            )
            if flip:
                block = jnp.concatenate([block, block], axis=0).T[:BS]
            high = block.astype(bf16)
            blocks[slot, :, :LANES] = high
            blocks[slot, :, LANES:] = (block - high.astype(f32)).astype(bf16)
            return carry

        lax.fori_loop(0, STEP, one, 0, unroll=8)


def prepare(vals, count, flip):
    def at(step, count):
        return jnp.minimum(step, count[0] // STEP - 1)

    return pl.pallas_call(
        functools.partial(prepare_kernel, flip),
        out_shape=pltpu.HBM((SLOTS, BS, F), bf16),
        grid_spec=pltpu.PrefetchScalarGridSpec(
            num_scalar_prefetch=1,
            grid=(SLOTS // STEP,),
            in_specs=[pl.BlockSpec((STEP, BS * BS), lambda s, n: (at(s, n), 0))],
            out_specs=pl.BlockSpec((STEP, BS, F), lambda s, n: (at(s, n), 0, 0)),
            scratch_shapes=[pltpu.VMEM((STEP * 32, LANES), f32)],
        ),
        cost_estimate=pl.CostEstimate(flops=10**8, bytes_accessed=12 << 20, transcendentals=0),
        compiler_params=room(8),
        name="prepare_back" if flip else "prepare",
    )(count, pltpu.with_memory_space_constraint(vals, pltpu.HBM))


def aggregate_kernel(n_src, n_dst, *refs):
    source_at, target_at, count = refs[:3]
    blocks = refs[3]
    sources = refs[4 : 4 + n_src]
    targets = refs[4 + n_src : 4 + n_src + n_dst]
    held, split, total, in_sems, out_sems = refs[4 + n_src + n_dst :]
    step = pl.program_id(0)
    in_rows = sources[0].shape[0]
    out_rows = targets[0].shape[0]

    def load(n):
        return pltpu.make_async_copy(
            sources[n], held.at[pl.ds(n * in_rows, in_rows)], in_sems.at[n]
        )

    def keep(n):
        return pltpu.make_async_copy(
            total.at[pl.ds(n * out_rows, out_rows)], targets[n], out_sems.at[n]
        )

    @pl.when(step == 0)
    def _():
        for n in range(n_src):
            load(n).start()
        total[...] = jnp.zeros_like(total)
        per = in_rows // BS
        for n in range(n_src):
            load(n).wait()

            def one(k, carry):
                at = n * per + k
                rows = held[pl.ds(pl.multiple_of(at * BS, BS), BS), :]
                high = rows.astype(bf16)
                low = (rows - high.astype(f32)).astype(bf16)
                split[at, 0:BS, :] = high
                split[at, BS : 2 * BS, :] = low
                split[at, 2 * BS :, :] = high
                return carry

            lax.fori_loop(0, per, one, 0, unroll=2)

    @pl.when(step * STEP < count[0])
    def _():
        for slot in range(STEP):
            at = step * STEP + slot
            term = jnp.dot(
                blocks[slot][:, :DEPTH], split[source_at[at]], preferred_element_type=f32
            )
            into = pl.ds(pl.multiple_of(target_at[at] * BS, BS), BS)
            total[into, :] += term

    @pl.when(step == pl.num_programs(0) - 1)
    def _():
        for n in range(n_dst):
            keep(n).start()
        for n in range(n_dst):
            keep(n).wait()


def aggregate(blocks, sources, source_at, target_at, count, n_dst, out_rows):
    n_src = len(sources)
    total_in = sum(s.shape[0] for s in sources)
    steps = SLOTS // STEP
    return pl.pallas_call(
        functools.partial(aggregate_kernel, n_src, n_dst),
        out_shape=[jax.ShapeDtypeStruct((out_rows // n_dst, F), f32)] * n_dst,
        grid_spec=pltpu.PrefetchScalarGridSpec(
            num_scalar_prefetch=3,
            grid=(steps,),
            in_specs=[
                pl.BlockSpec(
                    (STEP, BS, F),
                    lambda s, a, b, n: (jnp.minimum(s, n[0] // STEP - 1), 0, 0),
                )
            ]
            + [anywhere()] * n_src,
            out_specs=[anywhere()] * n_dst,
            scratch_shapes=[
                pltpu.VMEM((total_in, F), f32),
                pltpu.VMEM((total_in // BS, DEPTH, F), bf16),
                pltpu.VMEM((out_rows, F), f32),
                pltpu.SemaphoreType.DMA((n_src,)),
                pltpu.SemaphoreType.DMA((n_dst,)),
            ],
        ),
        cost_estimate=pl.CostEstimate(
            flops=2 * SLOTS * BS * F * F, bytes_accessed=16 << 20, transcendentals=0
        ),
        compiler_params=room(16),
    )(
        source_at,
        target_at,
        count,
        pltpu.with_memory_space_constraint(blocks, pltpu.HBM),
        *sources,
    )


def middle_kernel(*refs):
    where, parts, (weight, bias, cotangent) = refs[0], refs[1:9], refs[9:12]
    output, grad_a, grad_b, sums, gives, hidden, turned, strip = refs[12:]
    half = NODE // 2
    hidden[:half] = parts[0][...] + parts[1][...] + parts[2][...] + parts[3][...]
    hidden[half:] = parts[4][...] + parts[5][...] + parts[6][...] + parts[7][...]
    for side in range(2):
        lanes = slice(side * LANES, (side + 1) * LANES)
        strip[side * NODE : (side + 1) * NODE] = cotangent[:, lanes]
        for q in range(NODE // BS):
            for odd in range(2):
                turned[pl.ds(q * BS + odd * 32, 32), lanes] = strip[
                    pl.ds(side * NODE + q * BS + odd, 32, stride=2), :
                ]
    rows = hidden[...]
    preact = jnp.dot(rows, weight[...], precision=precise, preferred_element_type=f32)
    preact = preact + bias[...]
    squashed = 1.0 / (1.0 + jnp.exp(-preact))
    grad_pre = turned[...] * squashed * (1.0 + preact * (1.0 - squashed))
    turned[...] = preact * squashed
    grad = lax.dot_general(
        grad_pre, weight[...], (((1,), (1,)), ((), ())), precision=precise,
        preferred_element_type=f32,
    )
    grad_a[...] = grad[:half]
    grad_b[...] = grad[half:]
    for side in range(2):
        lanes = slice(side * LANES, (side + 1) * LANES)
        for q in range(NODE // BS):
            for odd in range(2):
                strip[pl.ds(side * NODE + q * BS + odd, 32, stride=2), :] = turned[
                    pl.ds(q * BS + odd * 32, 32), lanes
                ]
        output[:, lanes] = strip[side * NODE : (side + 1) * NODE]
    turned[...] = jnp.dot(rows.T, grad_pre, precision=precise, preferred_element_type=f32)
    local_b = jnp.sum(grad_pre, axis=0, keepdims=True)
    for f in range(SIDE):
        ahead = ((where[0] + f) & 3) * 2
        for side, into in ((where[1], sums), (1 - where[1], gives)):
            at = pl.multiple_of((ahead + side) * 32, 32)
            into[f * W_ROWS : f * W_ROWS + 32, :] = turned[pl.ds(at, 32), :]
            into[f * W_ROWS + 32 : (f + 1) * W_ROWS, :] = jnp.broadcast_to(
                local_b, (W_ROWS - 32, F)
            )


def middle(parts, weight, bias, cotangent, where):
    return pl.pallas_call(
        middle_kernel,
        out_shape=[
            jax.ShapeDtypeStruct((NODE, F), f32),
            jax.ShapeDtypeStruct((NODE // 2, F), f32),
            jax.ShapeDtypeStruct((NODE // 2, F), f32),
            jax.ShapeDtypeStruct((SIDE * W_ROWS, F), f32),
            jax.ShapeDtypeStruct((SIDE * W_ROWS, F), f32),
        ],
        in_specs=[pl.BlockSpec(memory_space=pltpu.SMEM)] + [whole()] * 11,
        out_specs=[whole()] * 5,
        scratch_shapes=[pltpu.VMEM((NODE, F), f32)] * 2 + [pltpu.VMEM((2 * NODE, LANES), f32)],
        compiler_params=room(12),
        name="middle",
    )(where, *parts, weight, bias.reshape(1, F), cotangent)


def on_device(
    features,
    loader_perm,
    block_values,
    block_row,
    block_column,
    tile_count,
    weight,
    bias_vector,
    cotangent,
):
    row = lax.axis_index("row")
    col = lax.axis_index("col")
    my_y, my_x = row // SIDE, row % SIDE
    my_z, my_c = col // 2, col % 2
    count = tile_count.reshape(1)
    tile_rows = block_row.reshape(SLOTS)
    tile_columns = block_column.reshape(SLOTS)

    r_dev, r_q = tile_rows >> 2, tile_rows & 3
    r_y, r_x = r_dev >> 2, r_dev & 3
    c_dev, c_q = tile_columns >> 2, tile_columns & 3
    c_z, c_c = c_dev >> 1, c_dev & 1
    out_d, out_e = (r_x - my_x) & 3, (r_y - my_y) & 3
    in_d, in_e = (my_x - r_x) & 3, (my_y - r_y) & 3

    def row_slot(d, e):
        first = d * 8 + e * 2 + (r_q & 1)
        second = 32 + e * 8 + d * 2 + (r_q & 1)
        return jnp.where(r_q < 2, first, second)

    fwd_to = row_slot(out_d, out_e)
    bwd_from = row_slot(in_d, in_e)
    other = c_c ^ my_c
    fwd_from = (((my_z - c_z) & 3) * 2 + other) * 4 + c_q
    bwd_to = (other * 4 + ((c_z - my_z) & 3)) * 4 + c_q

    sent = pack(features, loader_perm)
    got = lax.all_to_all(sent, ("row", "col"), split_axis=0, concat_axis=0, tiled=True)
    vals = block_values.reshape(SLOTS, BS * BS)
    fwd_blocks = prepare(vals, count, False)
    got, fwd_blocks = lax.optimization_barrier((got, fwd_blocks))
    own = place(got)
    panel = [own] + [lax.ppermute(own, "col", col_hop(f, 0)) for f in (1, 2, 3)]
    sources = []
    for part in panel:
        sources += [part, lax.ppermute(part, "col", col_hop(0, 1))]

    half = list(aggregate(
        fwd_blocks, sources, fwd_from, fwd_to, count, 8, ROWS * NODE)
    )
    got_a = [lax.ppermute(half[d], "row", row_hop(0, d)) for d in (1, 2, 3)]
    got_b = [lax.ppermute(half[4 + e], "row", row_hop(e, 0)) for e in (1, 2, 3)]
    n = NODE // 2
    back_count, half[0] = lax.optimization_barrier((count, half[0]))
    bwd_blocks = prepare(vals, back_count, True)
    got_a[0], bwd_blocks = lax.optimization_barrier((got_a[0], bwd_blocks))

    def partial(own_part, got, k):
        cut = slice(k * n, (k + 1) * n)
        return own_part[cut] + got[0][cut] + got[1][cut] + got[2][cut]

    sum_a = [partial(half[0], got_a, k) for k in range(SIDE)]
    sum_b = [partial(half[4], got_b, k) for k in range(SIDE)]
    parts = [sum_a[0]] + [lax.ppermute(sum_a[e], "row", row_hop(e, 0)) for e in (1, 2, 3)]
    parts += [sum_b[0]] + [lax.ppermute(sum_b[d], "row", row_hop(0, d)) for d in (1, 2, 3)]

    output, grad_a, grad_b, sums, gives = middle(
        parts, weight, bias_vector, cotangent, jnp.stack([my_z, my_c])
    )

    near_a = [grad_a] + [lax.ppermute(grad_a, "row", row_hop(e, 0)) for e in (1, 2, 3)]
    near_b = [grad_b] + [lax.ppermute(grad_b, "row", row_hop(0, d)) for d in (1, 2, 3)]
    near_a = jnp.concatenate(near_a, axis=0)
    near_b = jnp.concatenate(near_b, axis=0)
    near_a, near_b = lax.optimization_barrier((near_a, near_b))
    far_a = [lax.ppermute(near_a, "row", row_hop(0, d)) for d in (1, 3, 2)]
    far_b = [lax.ppermute(near_b, "row", row_hop(e, 0)) for e in (1, 3, 2)]
    column = [near_a, far_a[0], far_a[2], far_a[1], near_b, far_b[0], far_b[2], far_b[1]]
    column = [pltpu.with_memory_space_constraint(part, pltpu.HBM) for part in column]

    sums = sums + lax.ppermute(gives, "col", col_hop(0, 1))
    sums = sums.reshape(SIDE, W_ROWS, F)
    got_w = [lax.ppermute(sums[f], "col", col_hop(f, 0)) for f in (1, 2, 3)]
    sums = sums[0] + got_w[0] + got_w[1] + got_w[2]
    sums = jnp.broadcast_to(sums[None], (ROWS, W_ROWS, F))
    bwd_from, sums = lax.optimization_barrier((bwd_from, sums))
    sums = lax.all_to_all(sums, "row", split_axis=0, concat_axis=0, tiled=True)
    keep, give = aggregate(bwd_blocks, column, bwd_from, bwd_to, count, 2, COLS * NODE)
    taken = lax.ppermute(give, "col", col_hop(0, 1))
    keep, sums = lax.optimization_barrier((keep, sums))
    sums_x = [
        keep[k * NODE : (k + 1) * NODE] + taken[k * NODE : (k + 1) * NODE] for k in range(SIDE)
    ]
    got_x = [lax.ppermute(sums_x[f], "col", col_hop(f, 0)) for f in (1, 2, 3)]
    norm_scale = 1.0 / math.sqrt(NODE * ROWS * COLS)
    sums = jnp.sum(sums, axis=0) * norm_scale
    sums = jnp.broadcast_to(sums[None], (COLS, W_ROWS, F))
    sums = lax.all_to_all(sums, "col", split_axis=0, concat_axis=0, tiled=True)
    grad_w = sums[:, :32].reshape(F, F)
    grad_bias = sums[0, 32]
    grad_x = sums_x[0] + got_x[0] + got_x[1] + got_x[2]
    return (output, grad_x, grad_w, grad_bias)


def solution(mesh):
    in_specs = (
        P(("row", "col"), None),
        P(("row", "col")),
        P("row", "col", None, None),
        P("row", "col", None),
        P("row", "col", None),
        P("row", "col"),
        P(),
        P(),
        P(("row", "col"), None),
    )
    out_specs = (P(("row", "col"), None), P(("row", "col"), None), P(), P())

    return jax.shard_map(
        on_device, mesh=mesh, in_specs=in_specs, out_specs=out_specs, check_vma=False
    )
```

```python
import functools
import math

import jax
import jax.numpy as jnp
from jax import lax
from jax.experimental import pallas as pl
from jax.experimental.pallas import tpu as pltpu
from jax.sharding import PartitionSpec as P

precise = lax.Precision.HIGHEST
F = 256
BS = 64
NODE = 256
SLOTS = 256
STEP = 32
DEPTH = 192
ROWS = 16
COLS = 8
SIDE = 4
LANES = 128
W_ROWS = 40


f32 = jnp.float32
bf16 = jnp.bfloat16


def room(mib):
    return pltpu.CompilerParams(vmem_limit_bytes=mib << 20)


def whole():
    return pl.BlockSpec(memory_space=pltpu.VMEM)


def anywhere():
    return pl.BlockSpec(memory_space=pl.ANY)


def row_hop(dy, dx):
    return [
        (y * SIDE + x, (y + dy) % SIDE * SIDE + (x + dx) % SIDE)
        for y in range(SIDE)
        for x in range(SIDE)
    ]


def col_hop(dz, dc):
    return [
        (z * 2 + c, (z + dz) % SIDE * 2 + (c + dc) % 2) for z in range(SIDE) for c in range(2)
    ]


def pack_kernel(features, perm_row, sent):
    owner_row = jnp.broadcast_to(lax.shift_right_logical(perm_row[...], 8), (NODE, NODE))
    owner_col = owner_row.astype(f32).T.astype(jnp.int32)
    first = lax.broadcasted_iota(jnp.int32, (NODE, NODE), 0)
    second = lax.broadcasted_iota(jnp.int32, (NODE, NODE), 1)
    earlier = (owner_col == owner_row) & (first < second)
    rank = jnp.sum(earlier.astype(f32), axis=0, keepdims=True).astype(jnp.int32)
    slot = owner_row[:1] * 2 + rank
    spot = (perm_row[...] & (NODE - 1)).astype(f32)
    rows = lax.broadcasted_iota(jnp.int32, (NODE // 2, NODE), 0)
    for n in range(2):
        chosen = (rows * 2 + n == slot).astype(f32)
        sent[:, n, :F] = jnp.dot(
            chosen, features[...], precision=precise, preferred_element_type=f32
        )
        spots = jnp.sum(chosen * spot, axis=1, keepdims=True)
        sent[:, n, F:] = jnp.broadcast_to(spots, (NODE // 2, LANES))


def pack(features, perm):
    return pl.pallas_call(
        pack_kernel,
        out_shape=jax.ShapeDtypeStruct((NODE // 2, 2, F + LANES), f32),
        in_specs=[whole()] * 2,
        out_specs=whole(),
        compiler_params=room(8),
        name="pack",
    )(pltpu.with_memory_space_constraint(features, pltpu.HBM), perm.reshape(1, NODE))


def place_kernel(got, own):
    second = lax.broadcasted_iota(jnp.int32, (NODE // 2, NODE), 1)
    chosen, rows = [], []
    for n in range(2):
        spot = got[:, n, F:].astype(jnp.int32)
        chosen.append((jnp.concatenate([spot, spot], axis=1) == second).astype(f32))
        rows.append(got[:, n, :F])
    chosen = jnp.concatenate(chosen, axis=0).T
    rows = jnp.concatenate(rows, axis=0)
    own[...] = jnp.dot(chosen, rows, precision=precise, preferred_element_type=f32)


def place(got):
    return pl.pallas_call(
        place_kernel,
        out_shape=jax.ShapeDtypeStruct((NODE, F), f32),
        in_specs=[whole()],
        out_specs=whole(),
        compiler_params=room(8),
        name="place",
    )(got)


def prepare_kernel(flip, count, vals, blocks, lines):
    @pl.when(pl.program_id(0) * STEP < count[0])
    def _():
        for group in range(STEP // 8):
            for tile in range(0, BS * BS // LANES, 8):
                square = jnp.stack(
                    [
                        vals[pl.ds(group * 8, 8), pl.ds((tile + t) * LANES, LANES)]
                        for t in range(8)
                    ]
                )
                square = jnp.transpose(square, (1, 0, 2))
                for slot in range(8):
                    lines[pl.ds((group * 8 + slot) * 32 + tile, 8), :] = square[slot]
        left = lax.broadcasted_iota(jnp.int32, (32, LANES), 1) < BS

        def one(slot, carry):
            pair = lines[pl.ds(pl.multiple_of(slot * 32, 32), 32), :]
            turned = pltpu.roll(pair, BS, 1)
            block = jnp.concatenate(
                [jnp.where(left, pair, turned), jnp.where(left, turned, pair)], axis=0
            )
            if flip:
                block = jnp.concatenate([block, block], axis=0).T[:BS]
            high = block.astype(bf16)
            blocks[slot, :, :LANES] = high
            blocks[slot, :, LANES:] = (block - high.astype(f32)).astype(bf16)
            return carry

        lax.fori_loop(0, STEP, one, 0, unroll=8)


def prepare(vals, count, flip):
    def at(step, count):
        return jnp.minimum(step, count[0] // STEP - 1)

    return pl.pallas_call(
        functools.partial(prepare_kernel, flip),
        out_shape=pltpu.HBM((SLOTS, BS, F), bf16),
        grid_spec=pltpu.PrefetchScalarGridSpec(
            num_scalar_prefetch=1,
            grid=(SLOTS // STEP,),
            in_specs=[pl.BlockSpec((STEP, BS * BS), lambda s, n: (at(s, n), 0))],
            out_specs=pl.BlockSpec((STEP, BS, F), lambda s, n: (at(s, n), 0, 0)),
            scratch_shapes=[pltpu.VMEM((STEP * 32, LANES), f32)],
        ),
        cost_estimate=pl.CostEstimate(flops=10**8, bytes_accessed=12 << 20, transcendentals=0),
        compiler_params=room(8),
        name="prepare_back" if flip else "prepare",
    )(count, pltpu.with_memory_space_constraint(vals, pltpu.HBM))


def aggregate_kernel(n_src, n_dst, *refs):
    source_at, target_at, count = refs[:3]
    blocks = refs[3]
    sources = refs[4 : 4 + n_src]
    targets = refs[4 + n_src : 4 + n_src + n_dst]
    held, split, total, in_sems, out_sems = refs[4 + n_src + n_dst :]
    step = pl.program_id(0)
    in_rows = sources[0].shape[0]
    out_rows = targets[0].shape[0]

    def load(n):
        return pltpu.make_async_copy(
            sources[n], held.at[pl.ds(n * in_rows, in_rows)], in_sems.at[n]
        )

    def keep(n):
        return pltpu.make_async_copy(
            total.at[pl.ds(n * out_rows, out_rows)], targets[n], out_sems.at[n]
        )

    @pl.when(step == 0)
    def _():
        for n in range(n_src):
            load(n).start()
        total[...] = jnp.zeros_like(total)
        per = in_rows // BS
        for n in range(n_src):
            load(n).wait()

            def one(k, carry):
                at = n * per + k
                rows = held[pl.ds(pl.multiple_of(at * BS, BS), BS), :]
                high = rows.astype(bf16)
                low = (rows - high.astype(f32)).astype(bf16)
                split[at, 0:BS, :] = high
                split[at, BS : 2 * BS, :] = low
                split[at, 2 * BS :, :] = high
                return carry

            lax.fori_loop(0, per, one, 0, unroll=2)

    @pl.when(step * STEP < count[0])
    def _():
        for slot in range(STEP):
            at = step * STEP + slot
            term = jnp.dot(
                blocks[slot][:, :DEPTH], split[source_at[at]], preferred_element_type=f32
            )
            into = pl.ds(pl.multiple_of(target_at[at] * BS, BS), BS)
            total[into, :] += term

    @pl.when(step == pl.num_programs(0) - 1)
    def _():
        for n in range(n_dst):
            keep(n).start()
        for n in range(n_dst):
            keep(n).wait()


def aggregate(blocks, sources, source_at, target_at, count, n_dst, out_rows):
    n_src = len(sources)
    total_in = sum(s.shape[0] for s in sources)
    steps = SLOTS // STEP
    return pl.pallas_call(
        functools.partial(aggregate_kernel, n_src, n_dst),
        out_shape=[jax.ShapeDtypeStruct((out_rows // n_dst, F), f32)] * n_dst,
        grid_spec=pltpu.PrefetchScalarGridSpec(
            num_scalar_prefetch=3,
            grid=(steps,),
            in_specs=[
                pl.BlockSpec(
                    (STEP, BS, F),
                    lambda s, a, b, n: (jnp.minimum(s, n[0] // STEP - 1), 0, 0),
                )
            ]
            + [anywhere()] * n_src,
            out_specs=[anywhere()] * n_dst,
            scratch_shapes=[
                pltpu.VMEM((total_in, F), f32),
                pltpu.VMEM((total_in // BS, DEPTH, F), bf16),
                pltpu.VMEM((out_rows, F), f32),
                pltpu.SemaphoreType.DMA((n_src,)),
                pltpu.SemaphoreType.DMA((n_dst,)),
            ],
        ),
        cost_estimate=pl.CostEstimate(
            flops=2 * SLOTS * BS * F * F, bytes_accessed=16 << 20, transcendentals=0
        ),
        compiler_params=room(16),
    )(
        source_at,
        target_at,
        count,
        pltpu.with_memory_space_constraint(blocks, pltpu.HBM),
        *sources,
    )


def middle_kernel(*refs):
    where, parts, (weight, bias, cotangent) = refs[0], refs[1:9], refs[9:12]
    output, grad_a, grad_b, sums, gives, hidden, turned, strip = refs[12:]
    half = NODE // 2
    hidden[:half] = parts[0][...] + parts[1][...] + parts[2][...] + parts[3][...]
    hidden[half:] = parts[4][...] + parts[5][...] + parts[6][...] + parts[7][...]
    for side in range(2):
        lanes = slice(side * LANES, (side + 1) * LANES)
        strip[side * NODE : (side + 1) * NODE] = cotangent[:, lanes]
        for q in range(NODE // BS):
            for odd in range(2):
                turned[pl.ds(q * BS + odd * 32, 32), lanes] = strip[
                    pl.ds(side * NODE + q * BS + odd, 32, stride=2), :
                ]
    rows = hidden[...]
    preact = jnp.dot(rows, weight[...], precision=precise, preferred_element_type=f32)
    preact = preact + bias[...]
    squashed = 1.0 / (1.0 + jnp.exp(-preact))
    grad_pre = turned[...] * squashed * (1.0 + preact * (1.0 - squashed))
    turned[...] = preact * squashed
    grad = lax.dot_general(
        grad_pre, weight[...], (((1,), (1,)), ((), ())), precision=precise,
        preferred_element_type=f32,
    )
    grad_a[...] = grad[:half]
    grad_b[...] = grad[half:]
    for side in range(2):
        lanes = slice(side * LANES, (side + 1) * LANES)
        for q in range(NODE // BS):
            for odd in range(2):
                strip[pl.ds(side * NODE + q * BS + odd, 32, stride=2), :] = turned[
                    pl.ds(q * BS + odd * 32, 32), lanes
                ]
        output[:, lanes] = strip[side * NODE : (side + 1) * NODE]
    turned[...] = jnp.dot(rows.T, grad_pre, precision=precise, preferred_element_type=f32)
    local_b = jnp.sum(grad_pre, axis=0, keepdims=True)
    for f in range(SIDE):
        ahead = ((where[0] + f) & 3) * 2
        for side, into in ((where[1], sums), (1 - where[1], gives)):
            at = pl.multiple_of((ahead + side) * 32, 32)
            into[f * W_ROWS : f * W_ROWS + 32, :] = turned[pl.ds(at, 32), :]
            into[f * W_ROWS + 32 : (f + 1) * W_ROWS, :] = jnp.broadcast_to(
                local_b, (W_ROWS - 32, F)
            )


def middle(parts, weight, bias, cotangent, where):
    return pl.pallas_call(
        middle_kernel,
        out_shape=[
            jax.ShapeDtypeStruct((NODE, F), f32),
            jax.ShapeDtypeStruct((NODE // 2, F), f32),
            jax.ShapeDtypeStruct((NODE // 2, F), f32),
            jax.ShapeDtypeStruct((SIDE * W_ROWS, F), f32),
            jax.ShapeDtypeStruct((SIDE * W_ROWS, F), f32),
        ],
        in_specs=[pl.BlockSpec(memory_space=pltpu.SMEM)] + [whole()] * 11,
        out_specs=[whole()] * 5,
        scratch_shapes=[pltpu.VMEM((NODE, F), f32)] * 2 + [pltpu.VMEM((2 * NODE, LANES), f32)],
        compiler_params=room(12),
        name="middle",
    )(where, *parts, weight, bias.reshape(1, F), cotangent)


def finish_kernel(where, *refs):
    pieces, sums, (grad_x, grad_w, grad_b) = refs[:4], refs[4:8], refs[8:]
    grad_x[...] = pieces[0][...] + pieces[1][...] + pieces[2][...] + pieces[3][...]
    scale = 1.0 / math.sqrt(NODE * ROWS * COLS)
    for f in range(SIDE):
        chip = ((where[0] - f) & 3) * 2
        for side in range(2):
            n = chip + (where[1] ^ side)
            rows = sums[f][side * W_ROWS : (side + 1) * W_ROWS, :] * scale
            grad_w[pl.ds(pl.multiple_of(n * 32, 32), 32), :] = rows[:32]

            @pl.when(n == 0)
            def _():
                grad_b[...] = rows[32:33]


def finish(pieces, sums, where):
    return pl.pallas_call(
        finish_kernel,
        out_shape=[
            jax.ShapeDtypeStruct((NODE, F), f32),
            jax.ShapeDtypeStruct((F, F), f32),
            jax.ShapeDtypeStruct((1, F), f32),
        ],
        in_specs=[pl.BlockSpec(memory_space=pltpu.SMEM)] + [whole()] * 8,
        out_specs=[whole()] * 3,
        compiler_params=room(8),
        name="finish",
    )(where, *pieces, *sums)


def on_device(
    features,
    loader_perm,
    block_values,
    block_row,
    block_column,
    tile_count,
    weight,
    bias_vector,
    cotangent,
):
    row = lax.axis_index("row")
    col = lax.axis_index("col")
    my_y, my_x = row // SIDE, row % SIDE
    my_z, my_c = col // 2, col % 2
    where = jnp.stack([my_z, my_c])
    count = tile_count.reshape(1)
    tile_rows = block_row.reshape(SLOTS)
    tile_columns = block_column.reshape(SLOTS)

    r_dev, r_q = tile_rows >> 2, tile_rows & 3
    r_y, r_x = r_dev >> 2, r_dev & 3
    c_dev, c_q = tile_columns >> 2, tile_columns & 3
    c_z, c_c = c_dev >> 1, c_dev & 1
    out_d, out_e = (r_x - my_x) & 3, (r_y - my_y) & 3
    in_d, in_e = (my_x - r_x) & 3, (my_y - r_y) & 3

    def row_slot(d, e):
        first = d * 8 + e * 2 + (r_q & 1)
        second = 32 + e * 8 + d * 2 + (r_q & 1)
        return jnp.where(r_q < 2, first, second)

    fwd_to = row_slot(out_d, out_e)
    bwd_from = row_slot(in_d, in_e)
    other = c_c ^ my_c
    fwd_from = (((my_z - c_z) & 3) * 2 + other) * 4 + c_q
    bwd_to = (other * 4 + ((c_z - my_z) & 3)) * 4 + c_q

    sent = pack(features, loader_perm)
    got = lax.all_to_all(sent, ("row", "col"), split_axis=0, concat_axis=0, tiled=True)
    vals = block_values.reshape(SLOTS, BS * BS)
    fwd_blocks = prepare(vals, count, False)
    got, fwd_blocks = lax.optimization_barrier((got, fwd_blocks))
    own = place(got)
    panel = [own] + [lax.ppermute(own, "col", col_hop(f, 0)) for f in (1, 2, 3)]
    sources = []
    for part in panel:
        sources += [part, lax.ppermute(part, "col", col_hop(0, 1))]

    half = list(aggregate(
        fwd_blocks, sources, fwd_from, fwd_to, count, 8, ROWS * NODE)
    )
    got_a = [lax.ppermute(half[d], "row", row_hop(0, d)) for d in (1, 2, 3)]
    got_b = [lax.ppermute(half[4 + e], "row", row_hop(e, 0)) for e in (1, 2, 3)]
    n = NODE // 2
    back_count, half[0] = lax.optimization_barrier((count, half[0]))
    bwd_blocks = prepare(vals, back_count, True)
    got_a[0], bwd_blocks = lax.optimization_barrier((got_a[0], bwd_blocks))

    def partial(own_part, got, k):
        cut = slice(k * n, (k + 1) * n)
        return own_part[cut] + got[0][cut] + got[1][cut] + got[2][cut]

    sum_a = [partial(half[0], got_a, k) for k in range(SIDE)]
    sum_b = [partial(half[4], got_b, k) for k in range(SIDE)]
    parts = [sum_a[0]] + [lax.ppermute(sum_a[e], "row", row_hop(e, 0)) for e in (1, 2, 3)]
    parts += [sum_b[0]] + [lax.ppermute(sum_b[d], "row", row_hop(0, d)) for d in (1, 2, 3)]

    output, grad_a, grad_b, sums, gives = middle(
        parts, weight, bias_vector, cotangent, where
    )

    near_a = [grad_a] + [lax.ppermute(grad_a, "row", row_hop(e, 0)) for e in (1, 2, 3)]
    near_b = [grad_b] + [lax.ppermute(grad_b, "row", row_hop(0, d)) for d in (1, 2, 3)]
    near_a = jnp.concatenate(near_a, axis=0)
    near_b = jnp.concatenate(near_b, axis=0)
    near_a, near_b = lax.optimization_barrier((near_a, near_b))
    far_a = [lax.ppermute(near_a, "row", row_hop(0, d)) for d in (1, 3, 2)]
    far_b = [lax.ppermute(near_b, "row", row_hop(e, 0)) for e in (1, 3, 2)]
    column = [near_a, far_a[0], far_a[2], far_a[1], near_b, far_b[0], far_b[2], far_b[1]]

    sums = sums + lax.ppermute(gives, "col", col_hop(0, 1))
    sums = sums.reshape(SIDE, W_ROWS, F)
    got_w = [lax.ppermute(sums[f], "col", col_hop(f, 0)) for f in (1, 2, 3)]
    sums = sums[0] + got_w[0] + got_w[1] + got_w[2]
    got_w = [lax.ppermute(sums, "row", row_hop(0, d)) for d in (1, 3, 2)]
    sums = (sums + got_w[2]) + (got_w[0] + got_w[1])
    bwd_from, sums = lax.optimization_barrier((bwd_from, sums))
    got_w = lax.ppermute(sums, "col", col_hop(0, 1))
    sums = jnp.concatenate([sums, got_w], axis=0)
    keep, give = aggregate(bwd_blocks, column, bwd_from, bwd_to, count, 2, COLS * NODE)
    taken = lax.ppermute(give, "col", col_hop(0, 1))
    got_w = [lax.ppermute(sums, "row", row_hop(e, 0)) for e in (1, 3, 2)]
    sums = (sums + got_w[2]) + (got_w[0] + got_w[1])
    sums_x = [
        keep[k * NODE : (k + 1) * NODE] + taken[k * NODE : (k + 1) * NODE] for k in range(SIDE)
    ]
    got_x = [lax.ppermute(sums_x[f], "col", col_hop(f, 0)) for f in (1, 2, 3)]
    got_w = [lax.ppermute(sums, "col", col_hop(f, 0)) for f in (1, 2, 3)]
    grad_x, grad_w, grad_bias = finish(sums_x[:1] + got_x, [sums] + got_w, where)
    return (output, grad_x, grad_w, grad_bias.reshape(F))


def solution(mesh):
    in_specs = (
        P(("row", "col"), None),
        P(("row", "col")),
        P("row", "col", None, None),
        P("row", "col", None),
        P("row", "col", None),
        P("row", "col"),
        P(),
        P(),
        P(("row", "col"), None),
    )
    out_specs = (P(("row", "col"), None), P(("row", "col"), None), P(), P())

    return jax.shard_map(
        on_device, mesh=mesh, in_specs=in_specs, out_specs=out_specs, check_vma=False
    )
```

```python
import functools
import math

import jax
import jax.numpy as jnp
from jax import lax
from jax.experimental import pallas as pl
from jax.experimental.pallas import tpu as pltpu
from jax.sharding import PartitionSpec as P

precise = lax.Precision.HIGHEST
F = 256
BS = 64
NODE = 256
SLOTS = 256
STEP = 64
LEAST = 32
DEPTH = 192
ROWS = 16
COLS = 8
SIDE = 4
LANES = 128
W_ROWS = 40


f32 = jnp.float32
bf16 = jnp.bfloat16


def room(mib):
    return pltpu.CompilerParams(vmem_limit_bytes=mib << 20)


def whole():
    return pl.BlockSpec(memory_space=pltpu.VMEM)


def anywhere():
    return pl.BlockSpec(memory_space=pl.ANY)


def row_hop(dy, dx):
    return [
        (y * SIDE + x, (y + dy) % SIDE * SIDE + (x + dx) % SIDE)
        for y in range(SIDE)
        for x in range(SIDE)
    ]


def col_hop(dz, dc):
    return [
        (z * 2 + c, (z + dz) % SIDE * 2 + (c + dc) % 2) for z in range(SIDE) for c in range(2)
    ]


def pack_kernel(features, perm_row, sent):
    owner_row = jnp.broadcast_to(lax.shift_right_logical(perm_row[...], 8), (NODE, NODE))
    owner_col = owner_row.astype(f32).T.astype(jnp.int32)
    first = lax.broadcasted_iota(jnp.int32, (NODE, NODE), 0)
    second = lax.broadcasted_iota(jnp.int32, (NODE, NODE), 1)
    earlier = (owner_col == owner_row) & (first < second)
    rank = jnp.sum(earlier.astype(f32), axis=0, keepdims=True).astype(jnp.int32)
    slot = owner_row[:1] * 2 + rank
    spot = (perm_row[...] & (NODE - 1)).astype(f32)
    rows = lax.broadcasted_iota(jnp.int32, (NODE // 2, NODE), 0)
    for n in range(2):
        chosen = (rows * 2 + n == slot).astype(f32)
        sent[:, n, :F] = jnp.dot(
            chosen, features[...], precision=precise, preferred_element_type=f32
        )
        spots = jnp.sum(chosen * spot, axis=1, keepdims=True)
        sent[:, n, F:] = jnp.broadcast_to(spots, (NODE // 2, LANES))


def pack(features, perm):
    return pl.pallas_call(
        pack_kernel,
        out_shape=jax.ShapeDtypeStruct((NODE // 2, 2, F + LANES), f32),
        in_specs=[whole()] * 2,
        out_specs=whole(),
        compiler_params=room(8),
        name="pack",
    )(pltpu.with_memory_space_constraint(features, pltpu.HBM), perm.reshape(1, NODE))


def place_kernel(got, own):
    second = lax.broadcasted_iota(jnp.int32, (NODE // 2, NODE), 1)
    chosen, rows = [], []
    for n in range(2):
        spot = got[:, n, F:].astype(jnp.int32)
        chosen.append((jnp.concatenate([spot, spot], axis=1) == second).astype(f32))
        rows.append(got[:, n, :F])
    chosen = jnp.concatenate(chosen, axis=0).T
    rows = jnp.concatenate(rows, axis=0)
    own[...] = jnp.dot(chosen, rows, precision=precise, preferred_element_type=f32)


def place(got):
    return pl.pallas_call(
        place_kernel,
        out_shape=jax.ShapeDtypeStruct((NODE, F), f32),
        in_specs=[whole()],
        out_specs=whole(),
        compiler_params=room(8),
        name="place",
    )(got)


def prepare_kernel(flip, count, vals, blocks, lines):
    @pl.when(pl.program_id(0) * STEP < count[0])
    def _():
        for group in range(STEP // 8):
            for tile in range(0, BS * BS // LANES, 8):
                square = jnp.stack(
                    [
                        vals[pl.ds(group * 8, 8), pl.ds((tile + t) * LANES, LANES)]
                        for t in range(8)
                    ]
                )
                square = jnp.transpose(square, (1, 0, 2))
                for slot in range(8):
                    lines[pl.ds((group * 8 + slot) * 32 + tile, 8), :] = square[slot]
        left = lax.broadcasted_iota(jnp.int32, (32, LANES), 1) < BS

        def one(slot, carry):
            pair = lines[pl.ds(pl.multiple_of(slot * 32, 32), 32), :]
            turned = pltpu.roll(pair, BS, 1)
            block = jnp.concatenate(
                [jnp.where(left, pair, turned), jnp.where(left, turned, pair)], axis=0
            )
            if flip:
                block = jnp.concatenate([block, block], axis=0).T[:BS]
            high = block.astype(bf16)
            blocks[slot, :, :LANES] = high
            blocks[slot, :, LANES:] = (block - high.astype(f32)).astype(bf16)
            return carry

        lax.fori_loop(0, STEP, one, 0, unroll=8)


def prepare(vals, count, flip):
    def at(step, count):
        return jnp.minimum(step, jnp.maximum(count[0] // STEP, 1) - 1)

    return pl.pallas_call(
        functools.partial(prepare_kernel, flip),
        out_shape=pltpu.HBM((SLOTS, BS, F), bf16),
        grid_spec=pltpu.PrefetchScalarGridSpec(
            num_scalar_prefetch=1,
            grid=(SLOTS // STEP,),
            in_specs=[pl.BlockSpec((STEP, BS * BS), lambda s, n: (at(s, n), 0))],
            out_specs=pl.BlockSpec((STEP, BS, F), lambda s, n: (at(s, n), 0, 0)),
            scratch_shapes=[pltpu.VMEM((STEP * 32, LANES), f32)],
        ),
        cost_estimate=pl.CostEstimate(flops=10**8, bytes_accessed=12 << 20, transcendentals=0),
        compiler_params=room(12),
        name="prepare_back" if flip else "prepare",
    )(count, pltpu.with_memory_space_constraint(vals, pltpu.HBM))


def aggregate_kernel(n_src, n_dst, *refs):
    source_at, target_at, count = refs[:3]
    blocks = refs[3]
    sources = refs[4 : 4 + n_src]
    targets = refs[4 + n_src : 4 + n_src + n_dst]
    held, split, total, in_sems, out_sems = refs[4 + n_src + n_dst :]
    step = pl.program_id(0)
    in_rows = sources[0].shape[0]
    out_rows = targets[0].shape[0]

    def load(n):
        return pltpu.make_async_copy(
            sources[n], held.at[pl.ds(n * in_rows, in_rows)], in_sems.at[n]
        )

    def keep(n):
        return pltpu.make_async_copy(
            total.at[pl.ds(n * out_rows, out_rows)], targets[n], out_sems.at[n]
        )

    @pl.when(step == 0)
    def _():
        for n in range(n_src):
            load(n).start()
        total[...] = jnp.zeros_like(total)
        per = in_rows // BS
        for n in range(n_src):
            load(n).wait()

            def one(k, carry):
                at = n * per + k
                rows = held[pl.ds(pl.multiple_of(at * BS, BS), BS), :]
                high = rows.astype(bf16)
                low = (rows - high.astype(f32)).astype(bf16)
                split[at, 0:BS, :] = high
                split[at, BS : 2 * BS, :] = low
                split[at, 2 * BS :, :] = high
                return carry

            lax.fori_loop(0, per, one, 0, unroll=2)

    def slots(number):
        for slot in range(number):
            at = step * STEP + slot
            term = jnp.dot(
                blocks[slot][:, :DEPTH], split[source_at[at]], preferred_element_type=f32
            )
            into = pl.ds(pl.multiple_of(target_at[at] * BS, BS), BS)
            total[into, :] += term

    @pl.when((step + 1) * STEP <= count[0])
    def _():
        slots(STEP)

    @pl.when((step == 0) & (count[0] == LEAST))
    def _():
        slots(LEAST)

    @pl.when(step == pl.num_programs(0) - 1)
    def _():
        for n in range(n_dst):
            keep(n).start()
        for n in range(n_dst):
            keep(n).wait()


def aggregate(blocks, sources, source_at, target_at, count, n_dst, out_rows):
    n_src = len(sources)
    total_in = sum(s.shape[0] for s in sources)
    steps = SLOTS // STEP
    return pl.pallas_call(
        functools.partial(aggregate_kernel, n_src, n_dst),
        out_shape=[jax.ShapeDtypeStruct((out_rows // n_dst, F), f32)] * n_dst,
        grid_spec=pltpu.PrefetchScalarGridSpec(
            num_scalar_prefetch=3,
            grid=(steps,),
            in_specs=[
                pl.BlockSpec(
                    (STEP, BS, F),
                    lambda s, a, b, n: (
                        jnp.minimum(s, jnp.maximum(n[0] // STEP, 1) - 1), 0, 0
                    ),
                )
            ]
            + [anywhere()] * n_src,
            out_specs=[anywhere()] * n_dst,
            scratch_shapes=[
                pltpu.VMEM((total_in, F), f32),
                pltpu.VMEM((total_in // BS, DEPTH, F), bf16),
                pltpu.VMEM((out_rows, F), f32),
                pltpu.SemaphoreType.DMA((n_src,)),
                pltpu.SemaphoreType.DMA((n_dst,)),
            ],
        ),
        cost_estimate=pl.CostEstimate(
            flops=2 * SLOTS * BS * F * F, bytes_accessed=16 << 20, transcendentals=0
        ),
        compiler_params=room(18),
    )(
        source_at,
        target_at,
        count,
        pltpu.with_memory_space_constraint(blocks, pltpu.HBM),
        *sources,
    )


def middle_kernel(*refs):
    where, parts, (weight, bias, cotangent) = refs[0], refs[1:9], refs[9:12]
    output, grad_a, grad_b, sums, gives, hidden, turned, strip = refs[12:]
    half = NODE // 2
    hidden[:half] = parts[0][...] + parts[1][...] + parts[2][...] + parts[3][...]
    hidden[half:] = parts[4][...] + parts[5][...] + parts[6][...] + parts[7][...]
    for side in range(2):
        lanes = slice(side * LANES, (side + 1) * LANES)
        strip[side * NODE : (side + 1) * NODE] = cotangent[:, lanes]
        for q in range(NODE // BS):
            for odd in range(2):
                turned[pl.ds(q * BS + odd * 32, 32), lanes] = strip[
                    pl.ds(side * NODE + q * BS + odd, 32, stride=2), :
                ]
    rows = hidden[...]
    preact = jnp.dot(rows, weight[...], precision=precise, preferred_element_type=f32)
    preact = preact + bias[...]
    squashed = 1.0 / (1.0 + jnp.exp(-preact))
    grad_pre = turned[...] * squashed * (1.0 + preact * (1.0 - squashed))
    turned[...] = preact * squashed
    grad = lax.dot_general(
        grad_pre, weight[...], (((1,), (1,)), ((), ())), precision=precise,
        preferred_element_type=f32,
    )
    grad_a[...] = grad[:half]
    grad_b[...] = grad[half:]
    for side in range(2):
        lanes = slice(side * LANES, (side + 1) * LANES)
        for q in range(NODE // BS):
            for odd in range(2):
                strip[pl.ds(side * NODE + q * BS + odd, 32, stride=2), :] = turned[
                    pl.ds(q * BS + odd * 32, 32), lanes
                ]
        output[:, lanes] = strip[side * NODE : (side + 1) * NODE]
    turned[...] = jnp.dot(rows.T, grad_pre, precision=precise, preferred_element_type=f32)
    local_b = jnp.sum(grad_pre, axis=0, keepdims=True)
    for f in range(SIDE):
        ahead = ((where[0] + f) & 3) * 2
        for side, into in ((where[1], sums), (1 - where[1], gives)):
            at = pl.multiple_of((ahead + side) * 32, 32)
            into[f * W_ROWS : f * W_ROWS + 32, :] = turned[pl.ds(at, 32), :]
            into[f * W_ROWS + 32 : (f + 1) * W_ROWS, :] = jnp.broadcast_to(
                local_b, (W_ROWS - 32, F)
            )


def middle(parts, weight, bias, cotangent, where):
    return pl.pallas_call(
        middle_kernel,
        out_shape=[
            jax.ShapeDtypeStruct((NODE, F), f32),
            jax.ShapeDtypeStruct((NODE // 2, F), f32),
            jax.ShapeDtypeStruct((NODE // 2, F), f32),
            jax.ShapeDtypeStruct((SIDE * W_ROWS, F), f32),
            jax.ShapeDtypeStruct((SIDE * W_ROWS, F), f32),
        ],
        in_specs=[pl.BlockSpec(memory_space=pltpu.SMEM)] + [whole()] * 11,
        out_specs=[whole()] * 5,
        scratch_shapes=[pltpu.VMEM((NODE, F), f32)] * 2 + [pltpu.VMEM((2 * NODE, LANES), f32)],
        compiler_params=room(12),
        name="middle",
    )(where, *parts, weight, bias.reshape(1, F), cotangent)


def finish_kernel(where, *refs):
    pieces, sums, (grad_x, grad_w, grad_b) = refs[:4], refs[4:8], refs[8:]
    grad_x[...] = pieces[0][...] + pieces[1][...] + pieces[2][...] + pieces[3][...]
    scale = 1.0 / math.sqrt(NODE * ROWS * COLS)
    for f in range(SIDE):
        chip = ((where[0] - f) & 3) * 2
        for side in range(2):
            n = chip + (where[1] ^ side)
            rows = sums[f][side * W_ROWS : (side + 1) * W_ROWS, :] * scale
            grad_w[pl.ds(pl.multiple_of(n * 32, 32), 32), :] = rows[:32]

            @pl.when(n == 0)
            def _():
                grad_b[...] = rows[32:33]


def finish(pieces, sums, where):
    return pl.pallas_call(
        finish_kernel,
        out_shape=[
            jax.ShapeDtypeStruct((NODE, F), f32),
            jax.ShapeDtypeStruct((F, F), f32),
            jax.ShapeDtypeStruct((1, F), f32),
        ],
        in_specs=[pl.BlockSpec(memory_space=pltpu.SMEM)] + [whole()] * 8,
        out_specs=[whole()] * 3,
        compiler_params=room(8),
        name="finish",
    )(where, *pieces, *sums)


def on_device(
    features,
    loader_perm,
    block_values,
    block_row,
    block_column,
    tile_count,
    weight,
    bias_vector,
    cotangent,
):
    row = lax.axis_index("row")
    col = lax.axis_index("col")
    my_y, my_x = row // SIDE, row % SIDE
    my_z, my_c = col // 2, col % 2
    where = jnp.stack([my_z, my_c])
    count = tile_count.reshape(1)
    tile_rows = block_row.reshape(SLOTS)
    tile_columns = block_column.reshape(SLOTS)

    r_dev, r_q = tile_rows >> 2, tile_rows & 3
    r_y, r_x = r_dev >> 2, r_dev & 3
    c_dev, c_q = tile_columns >> 2, tile_columns & 3
    c_z, c_c = c_dev >> 1, c_dev & 1
    out_d, out_e = (r_x - my_x) & 3, (r_y - my_y) & 3
    in_d, in_e = (my_x - r_x) & 3, (my_y - r_y) & 3

    def row_slot(d, e):
        first = d * 8 + e * 2 + (r_q & 1)
        second = 32 + e * 8 + d * 2 + (r_q & 1)
        return jnp.where(r_q < 2, first, second)

    fwd_to = row_slot(out_d, out_e)
    bwd_from = row_slot(in_d, in_e)
    other = c_c ^ my_c
    fwd_from = (((my_z - c_z) & 3) * 2 + other) * 4 + c_q
    bwd_to = (other * 4 + ((c_z - my_z) & 3)) * 4 + c_q

    sent = pack(features, loader_perm)
    got = lax.all_to_all(sent, ("row", "col"), split_axis=0, concat_axis=0, tiled=True)
    vals = block_values.reshape(SLOTS, BS * BS)
    fwd_blocks = prepare(vals, count, False)
    got, fwd_blocks = lax.optimization_barrier((got, fwd_blocks))
    own = place(got)
    panel = [own] + [lax.ppermute(own, "col", col_hop(f, 0)) for f in (1, 2, 3)]
    sources = []
    for part in panel:
        sources += [part, lax.ppermute(part, "col", col_hop(0, 1))]

    half = list(aggregate(
        fwd_blocks, sources, fwd_from, fwd_to, count, 8, ROWS * NODE)
    )
    got_a = [lax.ppermute(half[d], "row", row_hop(0, d)) for d in (1, 2, 3)]
    got_b = [lax.ppermute(half[4 + e], "row", row_hop(e, 0)) for e in (1, 2, 3)]
    n = NODE // 2
    back_count, half[0] = lax.optimization_barrier((count, half[0]))
    bwd_blocks = prepare(vals, back_count, True)
    got_a[0], bwd_blocks = lax.optimization_barrier((got_a[0], bwd_blocks))

    def partial(own_part, got, k):
        cut = slice(k * n, (k + 1) * n)
        return own_part[cut] + got[0][cut] + got[1][cut] + got[2][cut]

    sum_a = [partial(half[0], got_a, k) for k in range(SIDE)]
    sum_b = [partial(half[4], got_b, k) for k in range(SIDE)]
    parts = [sum_a[0]] + [lax.ppermute(sum_a[e], "row", row_hop(e, 0)) for e in (1, 2, 3)]
    parts += [sum_b[0]] + [lax.ppermute(sum_b[d], "row", row_hop(0, d)) for d in (1, 2, 3)]

    output, grad_a, grad_b, sums, gives = middle(
        parts, weight, bias_vector, cotangent, where
    )

    near_a = [grad_a] + [lax.ppermute(grad_a, "row", row_hop(e, 0)) for e in (1, 2, 3)]
    near_b = [grad_b] + [lax.ppermute(grad_b, "row", row_hop(0, d)) for d in (1, 2, 3)]
    near_a = jnp.concatenate(near_a, axis=0)
    near_b = jnp.concatenate(near_b, axis=0)
    near_a, near_b = lax.optimization_barrier((near_a, near_b))
    far_a = [lax.ppermute(near_a, "row", row_hop(0, d)) for d in (1, 3, 2)]
    far_b = [lax.ppermute(near_b, "row", row_hop(e, 0)) for e in (1, 3, 2)]
    column = [near_a, far_a[0], far_a[2], far_a[1], near_b, far_b[0], far_b[2], far_b[1]]

    sums = sums + lax.ppermute(gives, "col", col_hop(0, 1))
    sums = sums.reshape(SIDE, W_ROWS, F)
    got_w = [lax.ppermute(sums[f], "col", col_hop(f, 0)) for f in (1, 2, 3)]
    sums = sums[0] + got_w[0] + got_w[1] + got_w[2]
    got_w = [lax.ppermute(sums, "row", row_hop(0, d)) for d in (1, 3, 2)]
    sums = (sums + got_w[2]) + (got_w[0] + got_w[1])
    bwd_from, sums = lax.optimization_barrier((bwd_from, sums))
    got_w = lax.ppermute(sums, "col", col_hop(0, 1))
    sums = jnp.concatenate([sums, got_w], axis=0)
    keep, give = aggregate(bwd_blocks, column, bwd_from, bwd_to, count, 2, COLS * NODE)
    taken = lax.ppermute(give, "col", col_hop(0, 1))
    got_w = [lax.ppermute(sums, "row", row_hop(e, 0)) for e in (1, 3, 2)]
    sums = (sums + got_w[2]) + (got_w[0] + got_w[1])
    sums_x = [
        keep[k * NODE : (k + 1) * NODE] + taken[k * NODE : (k + 1) * NODE] for k in range(SIDE)
    ]
    got_x = [lax.ppermute(sums_x[f], "col", col_hop(f, 0)) for f in (1, 2, 3)]
    got_w = [lax.ppermute(sums, "col", col_hop(f, 0)) for f in (1, 2, 3)]
    grad_x, grad_w, grad_bias = finish(sums_x[:1] + got_x, [sums] + got_w, where)
    return (output, grad_x, grad_w, grad_bias.reshape(F))


def solution(mesh):
    in_specs = (
        P(("row", "col"), None),
        P(("row", "col")),
        P("row", "col", None, None),
        P("row", "col", None),
        P("row", "col", None),
        P("row", "col"),
        P(),
        P(),
        P(("row", "col"), None),
    )
    out_specs = (P(("row", "col"), None), P(("row", "col"), None), P(), P())

    return jax.shard_map(
        on_device, mesh=mesh, in_specs=in_specs, out_specs=out_specs, check_vma=False
    )
```

```python
import functools
import math

import jax
import jax.numpy as jnp
from jax import lax
from jax.experimental import pallas as pl
from jax.experimental.pallas import tpu as pltpu
from jax.sharding import PartitionSpec as P

precise = lax.Precision.HIGHEST
F = 256
BS = 64
NODE = 256
SLOTS = 256
STEP = 64
LEAST = 32
DEPTH = 192
ROWS = 16
COLS = 8
SIDE = 4
LANES = 128
W_ROWS = 40


f32 = jnp.float32
bf16 = jnp.bfloat16


def room(mib):
    return pltpu.CompilerParams(vmem_limit_bytes=mib << 20)


def whole():
    return pl.BlockSpec(memory_space=pltpu.VMEM)


def anywhere():
    return pl.BlockSpec(memory_space=pl.ANY)


def row_hop(dy, dx):
    return [
        (y * SIDE + x, (y + dy) % SIDE * SIDE + (x + dx) % SIDE)
        for y in range(SIDE)
        for x in range(SIDE)
    ]


def alternate(first, second):
    got = ([None] * 3, [None] * 3)
    for hop in (2, 1, 3):
        for side, send in enumerate((first, second)):
            if send is not None:
                got[side][hop - 1] = send(hop)
    return got


def col_hop(dz, dc):
    return [
        (z * 2 + c, (z + dz) % SIDE * 2 + (c + dc) % 2) for z in range(SIDE) for c in range(2)
    ]


def pack_kernel(features, perm_row, sent):
    owner_row = jnp.broadcast_to(lax.shift_right_logical(perm_row[...], 8), (NODE, NODE))
    owner_col = owner_row.astype(f32).T.astype(jnp.int32)
    first = lax.broadcasted_iota(jnp.int32, (NODE, NODE), 0)
    second = lax.broadcasted_iota(jnp.int32, (NODE, NODE), 1)
    earlier = (owner_col == owner_row) & (first < second)
    rank = jnp.sum(earlier.astype(f32), axis=0, keepdims=True).astype(jnp.int32)
    slot = owner_row[:1] * 2 + rank
    spot = (perm_row[...] & (NODE - 1)).astype(f32)
    rows = lax.broadcasted_iota(jnp.int32, (NODE // 2, NODE), 0)
    for n in range(2):
        chosen = (rows * 2 + n == slot).astype(f32)
        sent[:, n, :F] = jnp.dot(
            chosen, features[...], precision=precise, preferred_element_type=f32
        )
        spots = jnp.sum(chosen * spot, axis=1, keepdims=True)
        sent[:, n, F:] = jnp.broadcast_to(spots, (NODE // 2, LANES))


def pack(features, perm):
    return pl.pallas_call(
        pack_kernel,
        out_shape=jax.ShapeDtypeStruct((NODE // 2, 2, F + LANES), f32),
        in_specs=[whole()] * 2,
        out_specs=whole(),
        compiler_params=room(8),
        name="pack",
    )(pltpu.with_memory_space_constraint(features, pltpu.HBM), perm.reshape(1, NODE))


def place_kernel(got, own):
    second = lax.broadcasted_iota(jnp.int32, (NODE // 2, NODE), 1)
    chosen, rows = [], []
    for n in range(2):
        spot = got[:, n, F:].astype(jnp.int32)
        chosen.append((jnp.concatenate([spot, spot], axis=1) == second).astype(f32))
        rows.append(got[:, n, :F])
    chosen = jnp.concatenate(chosen, axis=0).T
    rows = jnp.concatenate(rows, axis=0)
    own[...] = jnp.dot(chosen, rows, precision=precise, preferred_element_type=f32)


def place(got):
    return pl.pallas_call(
        place_kernel,
        out_shape=jax.ShapeDtypeStruct((NODE, F), f32),
        in_specs=[whole()],
        out_specs=whole(),
        compiler_params=room(8),
        name="place",
    )(got)


def prepare_kernel(flip, count, vals, blocks, lines):
    @pl.when(pl.program_id(0) * STEP < count[0])
    def _():
        for group in range(STEP // 8):
            for tile in range(0, BS * BS // LANES, 8):
                square = jnp.stack(
                    [
                        vals[pl.ds(group * 8, 8), pl.ds((tile + t) * LANES, LANES)]
                        for t in range(8)
                    ]
                )
                square = jnp.transpose(square, (1, 0, 2))
                for slot in range(8):
                    lines[pl.ds((group * 8 + slot) * 32 + tile, 8), :] = square[slot]
        left = lax.broadcasted_iota(jnp.int32, (32, LANES), 1) < BS

        def one(slot, carry):
            pair = lines[pl.ds(pl.multiple_of(slot * 32, 32), 32), :]
            turned = pltpu.roll(pair, BS, 1)
            block = jnp.concatenate(
                [jnp.where(left, pair, turned), jnp.where(left, turned, pair)], axis=0
            )
            if flip:
                block = jnp.concatenate([block, block], axis=0).T[:BS]
            high = block.astype(bf16)
            blocks[slot, :, :LANES] = high
            blocks[slot, :, LANES:] = (block - high.astype(f32)).astype(bf16)
            return carry

        lax.fori_loop(0, STEP, one, 0, unroll=8)


def prepare(vals, count, flip):
    def at(step, count):
        return jnp.minimum(step, jnp.maximum(count[0] // STEP, 1) - 1)

    return pl.pallas_call(
        functools.partial(prepare_kernel, flip),
        out_shape=pltpu.HBM((SLOTS, BS, F), bf16),
        grid_spec=pltpu.PrefetchScalarGridSpec(
            num_scalar_prefetch=1,
            grid=(SLOTS // STEP,),
            in_specs=[pl.BlockSpec((STEP, BS * BS), lambda s, n: (at(s, n), 0))],
            out_specs=pl.BlockSpec((STEP, BS, F), lambda s, n: (at(s, n), 0, 0)),
            scratch_shapes=[pltpu.VMEM((STEP * 32, LANES), f32)],
        ),
        cost_estimate=pl.CostEstimate(flops=10**8, bytes_accessed=12 << 20, transcendentals=0),
        compiler_params=room(12),
        name="prepare_back" if flip else "prepare",
    )(count, pltpu.with_memory_space_constraint(vals, pltpu.HBM))


def aggregate_kernel(n_src, n_dst, *refs):
    source_at, target_at, count = refs[:3]
    blocks = refs[3]
    sources = refs[4 : 4 + n_src]
    targets = refs[4 + n_src : 4 + n_src + n_dst]
    held, split, total, in_sems, out_sems = refs[4 + n_src + n_dst :]
    step = pl.program_id(0)
    in_rows = sources[0].shape[0]
    out_rows = targets[0].shape[0]

    def load(n):
        return pltpu.make_async_copy(
            sources[n], held.at[pl.ds(n * in_rows, in_rows)], in_sems.at[n]
        )

    def keep(n):
        return pltpu.make_async_copy(
            total.at[pl.ds(n * out_rows, out_rows)], targets[n], out_sems.at[n]
        )

    @pl.when(step == 0)
    def _():
        for n in range(n_src):
            load(n).start()
        total[...] = jnp.zeros_like(total)
        per = in_rows // BS
        for n in range(n_src):
            load(n).wait()

            def one(k, carry):
                at = n * per + k
                rows = held[pl.ds(pl.multiple_of(at * BS, BS), BS), :]
                high = rows.astype(bf16)
                low = (rows - high.astype(f32)).astype(bf16)
                split[at, 0:BS, :] = high
                split[at, BS : 2 * BS, :] = low
                split[at, 2 * BS :, :] = high
                return carry

            lax.fori_loop(0, per, one, 0, unroll=2)

    def slots(number):
        for slot in range(number):
            at = step * STEP + slot
            term = jnp.dot(
                blocks[slot][:, :DEPTH], split[source_at[at]], preferred_element_type=f32
            )
            into = pl.ds(pl.multiple_of(target_at[at] * BS, BS), BS)
            total[into, :] += term

    @pl.when((step + 1) * STEP <= count[0])
    def _():
        slots(STEP)

    @pl.when((step == 0) & (count[0] == LEAST))
    def _():
        slots(LEAST)

    @pl.when(step == pl.num_programs(0) - 1)
    def _():
        for n in range(n_dst):
            keep(n).start()
        for n in range(n_dst):
            keep(n).wait()


def aggregate(blocks, sources, source_at, target_at, count, n_dst, out_rows):
    n_src = len(sources)
    total_in = sum(s.shape[0] for s in sources)
    steps = SLOTS // STEP
    return pl.pallas_call(
        functools.partial(aggregate_kernel, n_src, n_dst),
        out_shape=[jax.ShapeDtypeStruct((out_rows // n_dst, F), f32)] * n_dst,
        grid_spec=pltpu.PrefetchScalarGridSpec(
            num_scalar_prefetch=3,
            grid=(steps,),
            in_specs=[
                pl.BlockSpec(
                    (STEP, BS, F),
                    lambda s, a, b, n: (
                        jnp.minimum(s, jnp.maximum(n[0] // STEP, 1) - 1), 0, 0
                    ),
                )
            ]
            + [anywhere()] * n_src,
            out_specs=[anywhere()] * n_dst,
            scratch_shapes=[
                pltpu.VMEM((total_in, F), f32),
                pltpu.VMEM((total_in // BS, DEPTH, F), bf16),
                pltpu.VMEM((out_rows, F), f32),
                pltpu.SemaphoreType.DMA((n_src,)),
                pltpu.SemaphoreType.DMA((n_dst,)),
            ],
        ),
        cost_estimate=pl.CostEstimate(
            flops=2 * SLOTS * BS * F * F, bytes_accessed=16 << 20, transcendentals=0
        ),
        compiler_params=room(18),
    )(
        source_at,
        target_at,
        count,
        pltpu.with_memory_space_constraint(blocks, pltpu.HBM),
        *sources,
    )


def middle_kernel(*refs):
    where, parts, (weight, bias, cotangent) = refs[0], refs[1:9], refs[9:12]
    output, grad_a, grad_b, sums, gives, hidden, turned, strip = refs[12:]
    half = NODE // 2
    hidden[:half] = parts[0][...] + parts[1][...] + parts[2][...] + parts[3][...]
    hidden[half:] = parts[4][...] + parts[5][...] + parts[6][...] + parts[7][...]
    for side in range(2):
        lanes = slice(side * LANES, (side + 1) * LANES)
        strip[side * NODE : (side + 1) * NODE] = cotangent[:, lanes]
        for q in range(NODE // BS):
            for odd in range(2):
                turned[pl.ds(q * BS + odd * 32, 32), lanes] = strip[
                    pl.ds(side * NODE + q * BS + odd, 32, stride=2), :
                ]
    rows = hidden[...]
    preact = jnp.dot(rows, weight[...], precision=precise, preferred_element_type=f32)
    preact = preact + bias[...]
    squashed = 1.0 / (1.0 + jnp.exp(-preact))
    grad_pre = turned[...] * squashed * (1.0 + preact * (1.0 - squashed))
    turned[...] = preact * squashed
    grad = lax.dot_general(
        grad_pre, weight[...], (((1,), (1,)), ((), ())), precision=precise,
        preferred_element_type=f32,
    )
    grad_a[...] = grad[:half]
    grad_b[...] = grad[half:]
    for side in range(2):
        lanes = slice(side * LANES, (side + 1) * LANES)
        for q in range(NODE // BS):
            for odd in range(2):
                strip[pl.ds(side * NODE + q * BS + odd, 32, stride=2), :] = turned[
                    pl.ds(q * BS + odd * 32, 32), lanes
                ]
        output[:, lanes] = strip[side * NODE : (side + 1) * NODE]
    turned[...] = jnp.dot(rows.T, grad_pre, precision=precise, preferred_element_type=f32)
    local_b = jnp.sum(grad_pre, axis=0, keepdims=True)
    for f in range(SIDE):
        ahead = ((where[0] + f) & 3) * 2
        for side, into in ((where[1], sums), (1 - where[1], gives)):
            at = pl.multiple_of((ahead + side) * 32, 32)
            into[f * W_ROWS : f * W_ROWS + 32, :] = turned[pl.ds(at, 32), :]
            into[f * W_ROWS + 32 : (f + 1) * W_ROWS, :] = jnp.broadcast_to(
                local_b, (W_ROWS - 32, F)
            )


def middle(parts, weight, bias, cotangent, where):
    return pl.pallas_call(
        middle_kernel,
        out_shape=[
            jax.ShapeDtypeStruct((NODE, F), f32),
            jax.ShapeDtypeStruct((NODE // 2, F), f32),
            jax.ShapeDtypeStruct((NODE // 2, F), f32),
            jax.ShapeDtypeStruct((SIDE * W_ROWS, F), f32),
            jax.ShapeDtypeStruct((SIDE * W_ROWS, F), f32),
        ],
        in_specs=[pl.BlockSpec(memory_space=pltpu.SMEM)] + [whole()] * 11,
        out_specs=[whole()] * 5,
        scratch_shapes=[pltpu.VMEM((NODE, F), f32)] * 2 + [pltpu.VMEM((2 * NODE, LANES), f32)],
        compiler_params=room(12),
        name="middle",
    )(where, *parts, weight, bias.reshape(1, F), cotangent)


def finish_kernel(where, *refs):
    pieces, sums, (grad_x, grad_w, grad_b) = refs[:4], refs[4:8], refs[8:]
    grad_x[...] = pieces[0][...] + pieces[1][...] + pieces[2][...] + pieces[3][...]
    scale = 1.0 / math.sqrt(NODE * ROWS * COLS)
    for f in range(SIDE):
        chip = ((where[0] - f) & 3) * 2
        for side in range(2):
            n = chip + (where[1] ^ side)
            rows = sums[f][side * W_ROWS : (side + 1) * W_ROWS, :] * scale
            grad_w[pl.ds(pl.multiple_of(n * 32, 32), 32), :] = rows[:32]

            @pl.when(n == 0)
            def _():
                grad_b[...] = rows[32:33]


def finish(pieces, sums, where):
    return pl.pallas_call(
        finish_kernel,
        out_shape=[
            jax.ShapeDtypeStruct((NODE, F), f32),
            jax.ShapeDtypeStruct((F, F), f32),
            jax.ShapeDtypeStruct((1, F), f32),
        ],
        in_specs=[pl.BlockSpec(memory_space=pltpu.SMEM)] + [whole()] * 8,
        out_specs=[whole()] * 3,
        compiler_params=room(8),
        name="finish",
    )(where, *pieces, *sums)


def on_device(
    features,
    loader_perm,
    block_values,
    block_row,
    block_column,
    tile_count,
    weight,
    bias_vector,
    cotangent,
):
    row = lax.axis_index("row")
    col = lax.axis_index("col")
    my_y, my_x = row // SIDE, row % SIDE
    my_z, my_c = col // 2, col % 2
    where = jnp.stack([my_z, my_c])
    count = tile_count.reshape(1)
    tile_rows = block_row.reshape(SLOTS)
    tile_columns = block_column.reshape(SLOTS)

    r_dev, r_q = tile_rows >> 2, tile_rows & 3
    r_y, r_x = r_dev >> 2, r_dev & 3
    c_dev, c_q = tile_columns >> 2, tile_columns & 3
    c_z, c_c = c_dev >> 1, c_dev & 1
    out_d, out_e = (r_x - my_x) & 3, (r_y - my_y) & 3
    in_d, in_e = (my_x - r_x) & 3, (my_y - r_y) & 3

    def row_slot(d, e):
        first = d * 8 + e * 2 + (r_q & 1)
        second = 32 + e * 8 + d * 2 + (r_q & 1)
        return jnp.where(r_q < 2, first, second)

    fwd_to = row_slot(out_d, out_e)
    bwd_from = row_slot(in_d, in_e)
    other = c_c ^ my_c
    fwd_from = (((my_z - c_z) & 3) * 2 + other) * 4 + c_q
    bwd_to = (other * 4 + ((c_z - my_z) & 3)) * 4 + c_q

    sent = pack(features, loader_perm)
    got = lax.all_to_all(sent, ("row", "col"), split_axis=0, concat_axis=0, tiled=True)
    vals = block_values.reshape(SLOTS, BS * BS)
    fwd_blocks = prepare(vals, count, False)
    got, fwd_blocks = lax.optimization_barrier((got, fwd_blocks))
    own = place(got)
    panel = [own] + alternate(lambda f: lax.ppermute(own, "col", col_hop(f, 0)), None)[0]
    sources = []
    for part in panel:
        sources += [part, lax.ppermute(part, "col", col_hop(0, 1))]

    half = list(aggregate(
        fwd_blocks, sources, fwd_from, fwd_to, count, 8, ROWS * NODE)
    )
    got_a, got_b = alternate(
        lambda d: lax.ppermute(half[d], "row", row_hop(0, d)),
        lambda e: lax.ppermute(half[4 + e], "row", row_hop(e, 0)),
    )
    n = NODE // 2
    back_count, half[0] = lax.optimization_barrier((count, half[0]))
    bwd_blocks = prepare(vals, back_count, True)
    got_a[0], bwd_blocks = lax.optimization_barrier((got_a[0], bwd_blocks))

    def partial(own_part, got, k):
        cut = slice(k * n, (k + 1) * n)
        return own_part[cut] + got[0][cut] + got[1][cut] + got[2][cut]

    sum_a = [partial(half[0], got_a, k) for k in range(SIDE)]
    sum_b = [partial(half[4], got_b, k) for k in range(SIDE)]
    rest_a = alternate(lambda e: lax.ppermute(sum_a[e], "row", row_hop(e, 0)), None)[0]
    rest_b = alternate(lambda d: lax.ppermute(sum_b[d], "row", row_hop(0, d)), None)[0]
    parts = [sum_a[0]] + rest_a + [sum_b[0]] + rest_b

    output, grad_a, grad_b, sums, gives = middle(
        parts, weight, bias_vector, cotangent, where
    )

    near_a, near_b = alternate(
        lambda e: lax.ppermute(grad_a, "row", row_hop(e, 0)),
        lambda d: lax.ppermute(grad_b, "row", row_hop(0, d)),
    )
    near_a = jnp.concatenate([grad_a] + near_a, axis=0)
    near_b = jnp.concatenate([grad_b] + near_b, axis=0)
    near_a, near_b = lax.optimization_barrier((near_a, near_b))
    far_a, far_b = alternate(
        lambda d: lax.ppermute(near_a, "row", row_hop(0, d)),
        lambda e: lax.ppermute(near_b, "row", row_hop(e, 0)),
    )
    column = [near_a] + far_a + [near_b] + far_b

    sums = sums + lax.ppermute(gives, "col", col_hop(0, 1))
    sums = sums.reshape(SIDE, W_ROWS, F)
    got_w = [lax.ppermute(sums[f], "col", col_hop(f, 0)) for f in (1, 2, 3)]
    sums = sums[0] + got_w[0] + got_w[1] + got_w[2]
    got_w = [lax.ppermute(sums, "row", row_hop(0, d)) for d in (1, 3, 2)]
    sums = (sums + got_w[2]) + (got_w[0] + got_w[1])
    bwd_from, sums = lax.optimization_barrier((bwd_from, sums))
    got_w = lax.ppermute(sums, "col", col_hop(0, 1))
    sums = jnp.concatenate([sums, got_w], axis=0)
    keep, give = aggregate(bwd_blocks, column, bwd_from, bwd_to, count, 2, COLS * NODE)
    taken = lax.ppermute(give, "col", col_hop(0, 1))
    got_w = [lax.ppermute(sums, "row", row_hop(e, 0)) for e in (1, 3, 2)]
    sums = (sums + got_w[2]) + (got_w[0] + got_w[1])
    sums_x = [
        keep[k * NODE : (k + 1) * NODE] + taken[k * NODE : (k + 1) * NODE] for k in range(SIDE)
    ]
    got_x, _ = alternate(lambda f: lax.ppermute(sums_x[f], "col", col_hop(f, 0)), None)
    got_w = [lax.ppermute(sums, "col", col_hop(f, 0)) for f in (1, 2, 3)]
    grad_x, grad_w, grad_bias = finish(sums_x[:1] + got_x, [sums] + got_w, where)
    return (output, grad_x, grad_w, grad_bias.reshape(F))


def solution(mesh):
    in_specs = (
        P(("row", "col"), None),
        P(("row", "col")),
        P("row", "col", None, None),
        P("row", "col", None),
        P("row", "col", None),
        P("row", "col"),
        P(),
        P(),
        P(("row", "col"), None),
    )
    out_specs = (P(("row", "col"), None), P(("row", "col"), None), P(), P())

    return jax.shard_map(
        on_device, mesh=mesh, in_specs=in_specs, out_specs=out_specs, check_vma=False
    )
```

```python
import functools
import math

import jax
import jax.numpy as jnp
from jax import lax
from jax.experimental import pallas as pl
from jax.experimental.pallas import tpu as pltpu
from jax.sharding import PartitionSpec as P

precise = lax.Precision.HIGHEST
F = 256
BS = 64
NODE = 256
SLOTS = 256
STEP = 64
LEAST = 32
DEPTH = 192
ROWS = 16
COLS = 8
SIDE = 4
LANES = 128
W_ROWS = 40


f32 = jnp.float32
bf16 = jnp.bfloat16


def room(mib):
    return pltpu.CompilerParams(vmem_limit_bytes=mib << 20)


def whole():
    return pl.BlockSpec(memory_space=pltpu.VMEM)


def anywhere():
    return pl.BlockSpec(memory_space=pl.ANY)


def row_hop(dy, dx):
    return [
        (y * SIDE + x, (y + dy) % SIDE * SIDE + (x + dx) % SIDE)
        for y in range(SIDE)
        for x in range(SIDE)
    ]


def alternate(first, second):
    got = ([None] * 3, [None] * 3)
    for hop in (2, 1, 3):
        for side, send in enumerate((first, second)):
            if send is not None:
                got[side][hop - 1] = send(hop)
    return got


def col_hop(dz, dc):
    return [
        (z * 2 + c, (z + dz) % SIDE * 2 + (c + dc) % 2) for z in range(SIDE) for c in range(2)
    ]


def pick(chosen, rows):
    chosen = chosen.astype(bf16)
    high = rows.astype(bf16)
    rest = rows - high.astype(f32)
    middle_part = rest.astype(bf16)
    low = (rest - middle_part.astype(f32)).astype(bf16)
    first, second, third = (
        jnp.dot(chosen, piece, preferred_element_type=f32) for piece in (high, middle_part, low)
    )
    return (first + second) + third


def pack_kernel(features, perm_row, sent):
    owner_row = jnp.broadcast_to(lax.shift_right_logical(perm_row[...], 8), (NODE, NODE))
    owner_col = owner_row.astype(f32).T.astype(jnp.int32)
    first = lax.broadcasted_iota(jnp.int32, (NODE, NODE), 0)
    second = lax.broadcasted_iota(jnp.int32, (NODE, NODE), 1)
    earlier = (owner_col == owner_row) & (first < second)
    rank = jnp.sum(earlier.astype(f32), axis=0, keepdims=True).astype(jnp.int32)
    slot = owner_row[:1] * 2 + rank
    spot = (perm_row[...] & (NODE - 1)).astype(f32)
    rows = lax.broadcasted_iota(jnp.int32, (NODE // 2, NODE), 0)
    for n in range(2):
        chosen = (rows * 2 + n == slot).astype(f32)
        sent[:, n, :F] = pick(chosen, features[...])
        spots = jnp.sum(chosen * spot, axis=1, keepdims=True)
        sent[:, n, F:] = jnp.broadcast_to(spots, (NODE // 2, LANES))


def pack(features, perm):
    return pl.pallas_call(
        pack_kernel,
        out_shape=jax.ShapeDtypeStruct((NODE // 2, 2, F + LANES), f32),
        in_specs=[whole()] * 2,
        out_specs=whole(),
        compiler_params=room(8),
        name="pack",
    )(
        pltpu.with_memory_space_constraint(features, pltpu.HBM),
        pltpu.with_memory_space_constraint(perm.reshape(1, NODE), pltpu.HBM),
    )


def place_kernel(got, own):
    second = lax.broadcasted_iota(jnp.int32, (NODE // 2, NODE), 1)
    chosen, rows = [], []
    for n in range(2):
        spot = got[:, n, F:].astype(jnp.int32)
        chosen.append((jnp.concatenate([spot, spot], axis=1) == second).astype(f32))
        rows.append(got[:, n, :F])
    chosen = jnp.concatenate(chosen, axis=0).T
    rows = jnp.concatenate(rows, axis=0)
    own[...] = pick(chosen, rows)


def place(got):
    return pl.pallas_call(
        place_kernel,
        out_shape=jax.ShapeDtypeStruct((NODE, F), f32),
        in_specs=[whole()],
        out_specs=whole(),
        compiler_params=room(8),
        name="place",
    )(got)


def prepare_kernel(flip, count, vals, blocks, lines):
    @pl.when(pl.program_id(0) * STEP < count[0])
    def _():
        for group in range(STEP // 8):
            for tile in range(0, BS * BS // LANES, 8):
                square = jnp.stack(
                    [
                        vals[pl.ds(group * 8, 8), pl.ds((tile + t) * LANES, LANES)]
                        for t in range(8)
                    ]
                )
                square = jnp.transpose(square, (1, 0, 2))
                for slot in range(8):
                    lines[pl.ds((group * 8 + slot) * 32 + tile, 8), :] = square[slot]
        left = lax.broadcasted_iota(jnp.int32, (32, LANES), 1) < BS

        def one(slot, carry):
            pair = lines[pl.ds(pl.multiple_of(slot * 32, 32), 32), :]
            turned = pltpu.roll(pair, BS, 1)
            block = jnp.concatenate(
                [jnp.where(left, pair, turned), jnp.where(left, turned, pair)], axis=0
            )
            if flip:
                block = jnp.concatenate([block, block], axis=0).T[:BS]
            high = block.astype(bf16)
            blocks[slot, :, :LANES] = high
            blocks[slot, :, LANES:] = (block - high.astype(f32)).astype(bf16)
            return carry

        lax.fori_loop(0, STEP, one, 0, unroll=8)


def prepare(vals, count, flip):
    def at(step, count):
        return jnp.minimum(step, jnp.maximum(count[0] // STEP, 1) - 1)

    return pl.pallas_call(
        functools.partial(prepare_kernel, flip),
        out_shape=pltpu.HBM((SLOTS, BS, F), bf16),
        grid_spec=pltpu.PrefetchScalarGridSpec(
            num_scalar_prefetch=1,
            grid=(SLOTS // STEP,),
            in_specs=[pl.BlockSpec((STEP, BS * BS), lambda s, n: (at(s, n), 0))],
            out_specs=pl.BlockSpec((STEP, BS, F), lambda s, n: (at(s, n), 0, 0)),
            scratch_shapes=[pltpu.VMEM((STEP * 32, LANES), f32)],
        ),
        cost_estimate=pl.CostEstimate(flops=10**8, bytes_accessed=12 << 20, transcendentals=0),
        compiler_params=room(12),
        name="prepare_back" if flip else "prepare",
    )(count, pltpu.with_memory_space_constraint(vals, pltpu.HBM))


def aggregate_kernel(n_src, n_dst, *refs):
    source_at, target_at, count = refs[:3]
    blocks = refs[3]
    sources = refs[4 : 4 + n_src]
    targets = refs[4 + n_src : 4 + n_src + n_dst]
    held, split, total, in_sems, out_sems = refs[4 + n_src + n_dst :]
    step = pl.program_id(0)
    in_rows = sources[0].shape[0]
    out_rows = targets[0].shape[0]

    def load(n):
        return pltpu.make_async_copy(
            sources[n], held.at[pl.ds(n * in_rows, in_rows)], in_sems.at[n]
        )

    def keep(n):
        return pltpu.make_async_copy(
            total.at[pl.ds(n * out_rows, out_rows)], targets[n], out_sems.at[n]
        )

    @pl.when(step == 0)
    def _():
        for n in range(n_src):
            load(n).start()
        total[...] = jnp.zeros_like(total)
        per = in_rows // BS
        for n in range(n_src):
            load(n).wait()

            def one(k, carry):
                at = n * per + k
                rows = held[pl.ds(pl.multiple_of(at * BS, BS), BS), :]
                high = rows.astype(bf16)
                low = (rows - high.astype(f32)).astype(bf16)
                split[at, 0:BS, :] = high
                split[at, BS : 2 * BS, :] = low
                split[at, 2 * BS :, :] = high
                return carry

            lax.fori_loop(0, per, one, 0, unroll=2)

    def slots(number):
        for slot in range(number):
            at = step * STEP + slot
            term = jnp.dot(
                blocks[slot][:, :DEPTH], split[source_at[at]], preferred_element_type=f32
            )
            into = pl.ds(pl.multiple_of(target_at[at] * BS, BS), BS)
            total[into, :] += term

    @pl.when((step + 1) * STEP <= count[0])
    def _():
        slots(STEP)

    @pl.when((step == 0) & (count[0] == LEAST))
    def _():
        slots(LEAST)

    @pl.when(step == pl.num_programs(0) - 1)
    def _():
        for n in range(n_dst):
            keep(n).start()
        for n in range(n_dst):
            keep(n).wait()


def aggregate(blocks, sources, source_at, target_at, count, n_dst, out_rows):
    n_src = len(sources)
    total_in = sum(s.shape[0] for s in sources)
    steps = SLOTS // STEP
    return pl.pallas_call(
        functools.partial(aggregate_kernel, n_src, n_dst),
        out_shape=[jax.ShapeDtypeStruct((out_rows // n_dst, F), f32)] * n_dst,
        grid_spec=pltpu.PrefetchScalarGridSpec(
            num_scalar_prefetch=3,
            grid=(steps,),
            in_specs=[
                pl.BlockSpec(
                    (STEP, BS, F),
                    lambda s, a, b, n: (
                        jnp.minimum(s, jnp.maximum(n[0] // STEP, 1) - 1), 0, 0
                    ),
                )
            ]
            + [anywhere()] * n_src,
            out_specs=[anywhere()] * n_dst,
            scratch_shapes=[
                pltpu.VMEM((total_in, F), f32),
                pltpu.VMEM((total_in // BS, DEPTH, F), bf16),
                pltpu.VMEM((out_rows, F), f32),
                pltpu.SemaphoreType.DMA((n_src,)),
                pltpu.SemaphoreType.DMA((n_dst,)),
            ],
        ),
        cost_estimate=pl.CostEstimate(
            flops=2 * SLOTS * BS * F * F, bytes_accessed=16 << 20, transcendentals=0
        ),
        compiler_params=room(18),
    )(
        source_at,
        target_at,
        count,
        pltpu.with_memory_space_constraint(blocks, pltpu.HBM),
        *sources,
    )


def middle_kernel(*refs):
    where, parts, (weight, bias, cotangent) = refs[0], refs[1:9], refs[9:12]
    output, grad_a, grad_b, sums, gives, hidden, turned, strip = refs[12:]
    half = NODE // 2
    hidden[:half] = parts[0][...] + parts[1][...] + parts[2][...] + parts[3][...]
    hidden[half:] = parts[4][...] + parts[5][...] + parts[6][...] + parts[7][...]
    for side in range(2):
        lanes = slice(side * LANES, (side + 1) * LANES)
        strip[side * NODE : (side + 1) * NODE] = cotangent[:, lanes]
        for q in range(NODE // BS):
            for odd in range(2):
                turned[pl.ds(q * BS + odd * 32, 32), lanes] = strip[
                    pl.ds(side * NODE + q * BS + odd, 32, stride=2), :
                ]
    rows = hidden[...]
    preact = jnp.dot(rows, weight[...], precision=precise, preferred_element_type=f32)
    preact = preact + bias[...]
    squashed = 1.0 / (1.0 + jnp.exp(-preact))
    grad_pre = turned[...] * squashed * (1.0 + preact * (1.0 - squashed))
    turned[...] = preact * squashed
    grad = lax.dot_general(
        grad_pre, weight[...], (((1,), (1,)), ((), ())), precision=precise,
        preferred_element_type=f32,
    )
    grad_a[...] = grad[:half]
    grad_b[...] = grad[half:]
    for side in range(2):
        lanes = slice(side * LANES, (side + 1) * LANES)
        for q in range(NODE // BS):
            for odd in range(2):
                strip[pl.ds(side * NODE + q * BS + odd, 32, stride=2), :] = turned[
                    pl.ds(q * BS + odd * 32, 32), lanes
                ]
        output[:, lanes] = strip[side * NODE : (side + 1) * NODE]
    turned[...] = jnp.dot(rows.T, grad_pre, precision=precise, preferred_element_type=f32)
    local_b = jnp.sum(grad_pre, axis=0, keepdims=True)
    for f in range(SIDE):
        ahead = ((where[0] + f) & 3) * 2
        for side, into in ((where[1], sums), (1 - where[1], gives)):
            at = pl.multiple_of((ahead + side) * 32, 32)
            into[f * W_ROWS : f * W_ROWS + 32, :] = turned[pl.ds(at, 32), :]
            into[f * W_ROWS + 32 : (f + 1) * W_ROWS, :] = jnp.broadcast_to(
                local_b, (W_ROWS - 32, F)
            )


def middle(parts, weight, bias, cotangent, where):
    return pl.pallas_call(
        middle_kernel,
        out_shape=[
            jax.ShapeDtypeStruct((NODE, F), f32),
            jax.ShapeDtypeStruct((NODE // 2, F), f32),
            jax.ShapeDtypeStruct((NODE // 2, F), f32),
            jax.ShapeDtypeStruct((SIDE * W_ROWS, F), f32),
            jax.ShapeDtypeStruct((SIDE * W_ROWS, F), f32),
        ],
        in_specs=[pl.BlockSpec(memory_space=pltpu.SMEM)] + [whole()] * 11,
        out_specs=[whole()] * 5,
        scratch_shapes=[pltpu.VMEM((NODE, F), f32)] * 2 + [pltpu.VMEM((2 * NODE, LANES), f32)],
        compiler_params=room(12),
        name="middle",
    )(where, *parts, weight, bias.reshape(1, F), cotangent)


def finish_kernel(where, *refs):
    pieces, sums, (grad_x, grad_w, grad_b) = refs[:4], refs[4:8], refs[8:]
    grad_x[...] = pieces[0][...] + pieces[1][...] + pieces[2][...] + pieces[3][...]
    scale = 1.0 / math.sqrt(NODE * ROWS * COLS)
    for f in range(SIDE):
        chip = ((where[0] - f) & 3) * 2
        for side in range(2):
            n = chip + (where[1] ^ side)
            rows = sums[f][side * W_ROWS : (side + 1) * W_ROWS, :] * scale
            grad_w[pl.ds(pl.multiple_of(n * 32, 32), 32), :] = rows[:32]

            @pl.when(n == 0)
            def _():
                grad_b[...] = rows[32:33]


def finish(pieces, sums, where):
    return pl.pallas_call(
        finish_kernel,
        out_shape=[
            jax.ShapeDtypeStruct((NODE, F), f32),
            jax.ShapeDtypeStruct((F, F), f32),
            jax.ShapeDtypeStruct((1, F), f32),
        ],
        in_specs=[pl.BlockSpec(memory_space=pltpu.SMEM)] + [whole()] * 8,
        out_specs=[whole()] * 3,
        compiler_params=room(8),
        name="finish",
    )(where, *pieces, *sums)


def on_device(
    features,
    loader_perm,
    block_values,
    block_row,
    block_column,
    tile_count,
    weight,
    bias_vector,
    cotangent,
):
    row = lax.axis_index("row")
    col = lax.axis_index("col")
    my_y, my_x = row // SIDE, row % SIDE
    my_z, my_c = col // 2, col % 2
    where = jnp.stack([my_z, my_c])
    count = tile_count.reshape(1)
    tile_rows = block_row.reshape(SLOTS)
    tile_columns = block_column.reshape(SLOTS)

    r_dev, r_q = tile_rows >> 2, tile_rows & 3
    r_y, r_x = r_dev >> 2, r_dev & 3
    c_dev, c_q = tile_columns >> 2, tile_columns & 3
    c_z, c_c = c_dev >> 1, c_dev & 1
    out_d, out_e = (r_x - my_x) & 3, (r_y - my_y) & 3
    in_d, in_e = (my_x - r_x) & 3, (my_y - r_y) & 3

    def row_slot(d, e):
        first = d * 8 + e * 2 + (r_q & 1)
        second = 32 + e * 8 + d * 2 + (r_q & 1)
        return jnp.where(r_q < 2, first, second)

    fwd_to = row_slot(out_d, out_e)
    bwd_from = row_slot(in_d, in_e)
    other = c_c ^ my_c
    fwd_from = (((my_z - c_z) & 3) * 2 + other) * 4 + c_q
    bwd_to = (other * 4 + ((c_z - my_z) & 3)) * 4 + c_q

    sent = pack(features, loader_perm)
    got = lax.all_to_all(sent, ("row", "col"), split_axis=0, concat_axis=0, tiled=True)
    vals = block_values.reshape(SLOTS, BS * BS)
    own = place(got)
    fwd_blocks = prepare(vals, count, False)
    panel = [own] + alternate(lambda f: lax.ppermute(own, "col", col_hop(f, 0)), None)[0]
    sources = []
    for part in panel:
        sources += [part, lax.ppermute(part, "col", col_hop(0, 1))]

    half = list(aggregate(
        fwd_blocks, sources, fwd_from, fwd_to, count, 8, ROWS * NODE)
    )
    got_a, got_b = alternate(
        lambda d: lax.ppermute(half[d], "row", row_hop(0, d)),
        lambda e: lax.ppermute(half[4 + e], "row", row_hop(e, 0)),
    )
    n = NODE // 2
    back_count, half[0] = lax.optimization_barrier((count, half[0]))
    bwd_blocks = prepare(vals, back_count, True)
    got_a[0], bwd_blocks = lax.optimization_barrier((got_a[0], bwd_blocks))

    def partial(own_part, got, k):
        cut = slice(k * n, (k + 1) * n)
        return own_part[cut] + got[0][cut] + got[1][cut] + got[2][cut]

    sum_a = [partial(half[0], got_a, k) for k in range(SIDE)]
    sum_b = [partial(half[4], got_b, k) for k in range(SIDE)]
    rest_a = alternate(lambda e: lax.ppermute(sum_a[e], "row", row_hop(e, 0)), None)[0]
    rest_b = alternate(lambda d: lax.ppermute(sum_b[d], "row", row_hop(0, d)), None)[0]
    parts = [sum_a[0]] + rest_a + [sum_b[0]] + rest_b

    output, grad_a, grad_b, sums, gives = middle(
        parts, weight, bias_vector, cotangent, where
    )

    near_a, near_b = alternate(
        lambda e: lax.ppermute(grad_a, "row", row_hop(e, 0)),
        lambda d: lax.ppermute(grad_b, "row", row_hop(0, d)),
    )
    near_a = jnp.concatenate([grad_a] + near_a, axis=0)
    near_b = jnp.concatenate([grad_b] + near_b, axis=0)
    got_w = lax.ppermute(gives, "col", col_hop(0, 1))
    near_a, near_b, got_w = lax.optimization_barrier((near_a, near_b, got_w))
    far_a, far_b = alternate(
        lambda d: lax.ppermute(near_a, "row", row_hop(0, d)),
        lambda e: lax.ppermute(near_b, "row", row_hop(e, 0)),
    )
    column = [near_a] + far_a + [near_b] + far_b

    sums = sums + got_w
    sums = sums.reshape(SIDE, W_ROWS, F)
    got_w = [lax.ppermute(sums[f], "col", col_hop(f, 0)) for f in (1, 2, 3)]
    sums = sums[0] + got_w[0] + got_w[1] + got_w[2]
    got_w = [lax.ppermute(sums, "row", row_hop(0, d)) for d in (1, 3, 2)]
    sums = (sums + got_w[2]) + (got_w[0] + got_w[1])
    bwd_from, sums = lax.optimization_barrier((bwd_from, sums))
    got_w = lax.ppermute(sums, "col", col_hop(0, 1))
    sums = jnp.concatenate([sums, got_w], axis=0)
    keep, give = aggregate(bwd_blocks, column, bwd_from, bwd_to, count, 2, COLS * NODE)
    taken = lax.ppermute(give, "col", col_hop(0, 1))
    got_w = [lax.ppermute(sums, "row", row_hop(e, 0)) for e in (1, 3, 2)]
    sums = (sums + got_w[2]) + (got_w[0] + got_w[1])
    sums_x = [
        keep[k * NODE : (k + 1) * NODE] + taken[k * NODE : (k + 1) * NODE] for k in range(SIDE)
    ]
    got_x, _ = alternate(lambda f: lax.ppermute(sums_x[f], "col", col_hop(f, 0)), None)
    got_w = [lax.ppermute(sums, "col", col_hop(f, 0)) for f in (1, 2, 3)]
    grad_x, grad_w, grad_bias = finish(sums_x[:1] + got_x, [sums] + got_w, where)
    return (output, grad_x, grad_w, grad_bias.reshape(F))


def solution(mesh):
    in_specs = (
        P(("row", "col"), None),
        P(("row", "col")),
        P("row", "col", None, None),
        P("row", "col", None),
        P("row", "col", None),
        P("row", "col"),
        P(),
        P(),
        P(("row", "col"), None),
    )
    out_specs = (P(("row", "col"), None), P(("row", "col"), None), P(), P())

    return jax.shard_map(
        on_device, mesh=mesh, in_specs=in_specs, out_specs=out_specs, check_vma=False
    )
```

```python
import functools
import math

import jax
import jax.numpy as jnp
from jax import lax
from jax.experimental import pallas as pl
from jax.experimental.pallas import tpu as pltpu
from jax.sharding import PartitionSpec as P

F = 256
BS = 64
NODE = 256
SLOTS = 256
STEP = 64
LEAST = 32
DEPTH = 192
ROWS = 16
COLS = 8
SIDE = 4
LANES = 128
W_ROWS = 40


f32 = jnp.float32
bf16 = jnp.bfloat16


def room(mib):
    return pltpu.CompilerParams(vmem_limit_bytes=mib << 20)


def whole():
    return pl.BlockSpec(memory_space=pltpu.VMEM)


def anywhere():
    return pl.BlockSpec(memory_space=pl.ANY)


def row_hop(dy, dx):
    return [
        (y * SIDE + x, (y + dy) % SIDE * SIDE + (x + dx) % SIDE)
        for y in range(SIDE)
        for x in range(SIDE)
    ]


def alternate(first, second):
    got = ([None] * 3, [None] * 3)
    for hop in (2, 1, 3):
        for side, send in enumerate((first, second)):
            if send is not None:
                got[side][hop - 1] = send(hop)
    return got


def col_hop(dz, dc):
    return [
        (z * 2 + c, (z + dz) % SIDE * 2 + (c + dc) % 2) for z in range(SIDE) for c in range(2)
    ]


def pick(chosen, rows):
    chosen = chosen.astype(bf16)
    high = rows.astype(bf16)
    rest = rows - high.astype(f32)
    middle_part = rest.astype(bf16)
    low = (rest - middle_part.astype(f32)).astype(bf16)
    first, second, third = (
        jnp.dot(chosen, piece, preferred_element_type=f32) for piece in (high, middle_part, low)
    )
    return (first + second) + third


def pack_kernel(features, perm_row, sent):
    owner_row = jnp.broadcast_to(lax.shift_right_logical(perm_row[...], 8), (NODE, NODE))
    owner_col = owner_row.astype(f32).T.astype(jnp.int32)
    first = lax.broadcasted_iota(jnp.int32, (NODE, NODE), 0)
    second = lax.broadcasted_iota(jnp.int32, (NODE, NODE), 1)
    earlier = (owner_col == owner_row) & (first < second)
    rank = jnp.sum(earlier.astype(f32), axis=0, keepdims=True).astype(jnp.int32)
    slot = owner_row[:1] * 2 + rank
    spot = (perm_row[...] & (NODE - 1)).astype(f32)
    rows = lax.broadcasted_iota(jnp.int32, (NODE // 2, NODE), 0)
    for n in range(2):
        chosen = (rows * 2 + n == slot).astype(f32)
        sent[:, n, :F] = pick(chosen, features[...])
        spots = jnp.sum(chosen * spot, axis=1, keepdims=True)
        sent[:, n, F:] = jnp.broadcast_to(spots, (NODE // 2, LANES))


def pack(features, perm):
    return pl.pallas_call(
        pack_kernel,
        out_shape=jax.ShapeDtypeStruct((NODE // 2, 2, F + LANES), f32),
        in_specs=[whole()] * 2,
        out_specs=whole(),
        compiler_params=room(8),
        name="pack",
    )(
        pltpu.with_memory_space_constraint(features, pltpu.HBM),
        pltpu.with_memory_space_constraint(perm.reshape(1, NODE), pltpu.HBM),
    )


def place_kernel(got, own):
    second = lax.broadcasted_iota(jnp.int32, (NODE // 2, NODE), 1)
    chosen, rows = [], []
    for n in range(2):
        spot = got[:, n, F:].astype(jnp.int32)
        chosen.append((jnp.concatenate([spot, spot], axis=1) == second).astype(f32))
        rows.append(got[:, n, :F])
    chosen = jnp.concatenate(chosen, axis=0).T
    rows = jnp.concatenate(rows, axis=0)
    own[...] = pick(chosen, rows)


def place(got):
    return pl.pallas_call(
        place_kernel,
        out_shape=jax.ShapeDtypeStruct((NODE, F), f32),
        in_specs=[whole()],
        out_specs=whole(),
        compiler_params=room(8),
        name="place",
    )(got)


def prepare_kernel(flip, count, vals, blocks, lines):
    @pl.when(pl.program_id(0) * STEP < count[0])
    def _():
        for group in range(STEP // 8):
            for tile in range(0, BS * BS // LANES, 8):
                square = jnp.stack(
                    [
                        vals[pl.ds(group * 8, 8), pl.ds((tile + t) * LANES, LANES)]
                        for t in range(8)
                    ]
                )
                square = jnp.transpose(square, (1, 0, 2))
                for slot in range(8):
                    lines[pl.ds((group * 8 + slot) * 32 + tile, 8), :] = square[slot]
        left = lax.broadcasted_iota(jnp.int32, (32, LANES), 1) < BS

        def one(slot, carry):
            pair = lines[pl.ds(pl.multiple_of(slot * 32, 32), 32), :]
            turned = pltpu.roll(pair, BS, 1)
            block = jnp.concatenate(
                [jnp.where(left, pair, turned), jnp.where(left, turned, pair)], axis=0
            )
            if flip:
                block = jnp.concatenate([block, block], axis=0).T[:BS]
            high = block.astype(bf16)
            blocks[slot, :, :LANES] = high
            blocks[slot, :, LANES:] = (block - high.astype(f32)).astype(bf16)
            return carry

        lax.fori_loop(0, STEP, one, 0, unroll=8)


def prepare(vals, count, flip):
    def at(step, count):
        return jnp.minimum(step, jnp.maximum(count[0] // STEP, 1) - 1)

    return pl.pallas_call(
        functools.partial(prepare_kernel, flip),
        out_shape=pltpu.HBM((SLOTS, BS, F), bf16),
        grid_spec=pltpu.PrefetchScalarGridSpec(
            num_scalar_prefetch=1,
            grid=(SLOTS // STEP,),
            in_specs=[pl.BlockSpec((STEP, BS * BS), lambda s, n: (at(s, n), 0))],
            out_specs=pl.BlockSpec((STEP, BS, F), lambda s, n: (at(s, n), 0, 0)),
            scratch_shapes=[pltpu.VMEM((STEP * 32, LANES), f32)],
        ),
        cost_estimate=pl.CostEstimate(flops=10**8, bytes_accessed=12 << 20, transcendentals=0),
        compiler_params=room(12),
        name="prepare_back" if flip else "prepare",
    )(count, pltpu.with_memory_space_constraint(vals, pltpu.HBM))


def aggregate_kernel(n_src, n_dst, source_at, target_at, count, blocks, *refs):
    sources, targets = refs[:n_src], refs[n_src : n_src + n_dst]
    held, split, total, stage, in_sems, out_sems, block_sems = refs[n_src + n_dst :]
    in_rows = sources[0].shape[0]
    out_rows = targets[0].shape[0]
    full = count[0] // STEP

    def fetch(step, slot):
        return pltpu.make_async_copy(
            blocks.at[pl.ds(step * STEP, STEP)], stage.at[slot], block_sems.at[slot]
        )

    def load(n):
        return pltpu.make_async_copy(
            sources[n], held.at[pl.ds(n * in_rows, in_rows)], in_sems.at[n]
        )

    def keep(n):
        return pltpu.make_async_copy(
            total.at[pl.ds(n * out_rows, out_rows)], targets[n], out_sems.at[n]
        )

    for n in range(n_src):
        load(n).start()
    fetch(0, 0).start()
    total[...] = jnp.zeros_like(total)
    per = in_rows // BS
    for n in range(n_src):
        load(n).wait()

        def one_block(k, carry):
            at = n * per + k
            rows = held[pl.ds(pl.multiple_of(at * BS, BS), BS), :]
            high = rows.astype(bf16)
            low = (rows - high.astype(f32)).astype(bf16)
            split[at, 0:BS, :] = high
            split[at, BS : 2 * BS, :] = low
            split[at, 2 * BS :, :] = high
            return carry

        lax.fori_loop(0, per, one_block, 0, unroll=2)

    def slots(step, place, number):
        for slot in range(number):
            at = step * STEP + slot
            term = jnp.dot(
                stage[place, slot][:, :DEPTH], split[source_at[at]], preferred_element_type=f32
            )
            into = pl.ds(pl.multiple_of(target_at[at] * BS, BS), BS)
            total[into, :] += term

    def one_step(step, carry):
        place = step & 1
        fetch(step, place).wait()

        @pl.when(step + 1 < full)
        def _():
            fetch(step + 1, 1 - place).start()

        slots(step, place, STEP)
        return carry

    lax.fori_loop(0, full, one_step, 0)

    @pl.when(count[0] == LEAST)
    def _():
        fetch(0, 0).wait()
        slots(0, 0, LEAST)

    for n in range(n_dst):
        keep(n).start()
    for n in range(n_dst):
        keep(n).wait()


def aggregate(blocks, sources, source_at, target_at, count, n_dst, out_rows):
    n_src = len(sources)
    total_in = sum(s.shape[0] for s in sources)
    return pl.pallas_call(
        functools.partial(aggregate_kernel, n_src, n_dst),
        out_shape=[jax.ShapeDtypeStruct((out_rows // n_dst, F), f32)] * n_dst,
        in_specs=[pl.BlockSpec(memory_space=pltpu.SMEM)] * 3 + [anywhere()] * (n_src + 1),
        out_specs=[anywhere()] * n_dst,
        scratch_shapes=[
            pltpu.VMEM((total_in, F), f32),
            pltpu.VMEM((total_in // BS, DEPTH, F), bf16),
            pltpu.VMEM((out_rows, F), f32),
            pltpu.VMEM((2, STEP, BS, F), bf16),
            pltpu.SemaphoreType.DMA((n_src,)),
            pltpu.SemaphoreType.DMA((n_dst,)),
            pltpu.SemaphoreType.DMA((2,)),
        ],
        cost_estimate=pl.CostEstimate(
            flops=2 * SLOTS * BS * F * F, bytes_accessed=16 << 20, transcendentals=0
        ),
        compiler_params=room(18),
    )(
        source_at,
        target_at,
        count,
        pltpu.with_memory_space_constraint(blocks, pltpu.HBM),
        *sources,
    )


def halves(rows):
    high = rows.astype(bf16)
    return high, (rows - high.astype(f32)).astype(bf16)


def product(left, right, dims):
    (a, b), (c, d) = halves(left), halves(right)

    def dot(u, v):
        return lax.dot_general(u, v, (dims, ((), ())), preferred_element_type=f32)

    return dot(a, c) + (dot(a, d) + dot(b, c))


def middle_kernel(*refs):
    where, parts, (weight, bias, cotangent) = refs[0], refs[1:9], refs[9:12]
    output, grad_a, grad_b, sums, gives, hidden, turned, strip = refs[12:]
    half = NODE // 2
    hidden[:half] = parts[0][...] + parts[1][...] + parts[2][...] + parts[3][...]
    hidden[half:] = parts[4][...] + parts[5][...] + parts[6][...] + parts[7][...]
    for side in range(2):
        lanes = slice(side * LANES, (side + 1) * LANES)
        strip[side * NODE : (side + 1) * NODE] = cotangent[:, lanes]
        for q in range(NODE // BS):
            for odd in range(2):
                turned[pl.ds(q * BS + odd * 32, 32), lanes] = strip[
                    pl.ds(side * NODE + q * BS + odd, 32, stride=2), :
                ]
    rows = hidden[...]
    preact = product(rows, weight[...], ((1,), (0,)))
    preact = preact + bias[...]
    squashed = 1.0 / (1.0 + jnp.exp(-preact))
    grad_pre = turned[...] * squashed * (1.0 + preact * (1.0 - squashed))
    turned[...] = preact * squashed
    grad = product(grad_pre, weight[...], ((1,), (1,)))
    grad_a[...] = grad[:half]
    grad_b[...] = grad[half:]
    for side in range(2):
        lanes = slice(side * LANES, (side + 1) * LANES)
        for q in range(NODE // BS):
            for odd in range(2):
                strip[pl.ds(side * NODE + q * BS + odd, 32, stride=2), :] = turned[
                    pl.ds(q * BS + odd * 32, 32), lanes
                ]
        output[:, lanes] = strip[side * NODE : (side + 1) * NODE]
    turned[...] = product(rows.T, grad_pre, ((1,), (0,)))
    local_b = jnp.sum(grad_pre, axis=0, keepdims=True)
    for f in range(SIDE):
        ahead = ((where[0] + f) & 3) * 2
        for side, into in ((where[1], sums), (1 - where[1], gives)):
            at = pl.multiple_of((ahead + side) * 32, 32)
            into[f * W_ROWS : f * W_ROWS + 32, :] = turned[pl.ds(at, 32), :]
            into[f * W_ROWS + 32 : (f + 1) * W_ROWS, :] = jnp.broadcast_to(
                local_b, (W_ROWS - 32, F)
            )


def middle(parts, weight, bias, cotangent, where):
    return pl.pallas_call(
        middle_kernel,
        out_shape=[
            jax.ShapeDtypeStruct((NODE, F), f32),
            jax.ShapeDtypeStruct((NODE // 2, F), f32),
            jax.ShapeDtypeStruct((NODE // 2, F), f32),
            jax.ShapeDtypeStruct((SIDE * W_ROWS, F), f32),
            jax.ShapeDtypeStruct((SIDE * W_ROWS, F), f32),
        ],
        in_specs=[pl.BlockSpec(memory_space=pltpu.SMEM)] + [whole()] * 11,
        out_specs=[whole()] * 5,
        scratch_shapes=[pltpu.VMEM((NODE, F), f32)] * 2 + [pltpu.VMEM((2 * NODE, LANES), f32)],
        compiler_params=room(12),
        name="middle",
    )(where, *parts, weight, bias.reshape(1, F), cotangent)


def finish_kernel(where, *refs):
    pieces, sums, (grad_x, grad_w, grad_b) = refs[:4], refs[4:8], refs[8:]
    grad_x[...] = pieces[0][...] + pieces[1][...] + pieces[2][...] + pieces[3][...]
    scale = 1.0 / math.sqrt(NODE * ROWS * COLS)
    for f in range(SIDE):
        chip = ((where[0] - f) & 3) * 2
        for side in range(2):
            n = chip + (where[1] ^ side)
            rows = sums[f][side * W_ROWS : (side + 1) * W_ROWS, :] * scale
            grad_w[pl.ds(pl.multiple_of(n * 32, 32), 32), :] = rows[:32]

            @pl.when(n == 0)
            def _():
                grad_b[...] = rows[32:33]


def finish(pieces, sums, where):
    return pl.pallas_call(
        finish_kernel,
        out_shape=[
            jax.ShapeDtypeStruct((NODE, F), f32),
            jax.ShapeDtypeStruct((F, F), f32),
            jax.ShapeDtypeStruct((1, F), f32),
        ],
        in_specs=[pl.BlockSpec(memory_space=pltpu.SMEM)] + [whole()] * 8,
        out_specs=[whole()] * 3,
        compiler_params=room(8),
        name="finish",
    )(where, *pieces, *sums)


def on_device(
    features,
    loader_perm,
    block_values,
    block_row,
    block_column,
    tile_count,
    weight,
    bias_vector,
    cotangent,
):
    row = lax.axis_index("row")
    col = lax.axis_index("col")
    my_y, my_x = row // SIDE, row % SIDE
    my_z, my_c = col // 2, col % 2
    where = jnp.stack([my_z, my_c])
    count = tile_count.reshape(1)
    tile_rows = block_row.reshape(SLOTS)
    tile_columns = block_column.reshape(SLOTS)

    r_dev, r_q = tile_rows >> 2, tile_rows & 3
    r_y, r_x = r_dev >> 2, r_dev & 3
    c_dev, c_q = tile_columns >> 2, tile_columns & 3
    c_z, c_c = c_dev >> 1, c_dev & 1
    out_d, out_e = (r_x - my_x) & 3, (r_y - my_y) & 3
    in_d, in_e = (my_x - r_x) & 3, (my_y - r_y) & 3

    def row_slot(d, e):
        first = d * 8 + e * 2 + (r_q & 1)
        second = 32 + e * 8 + d * 2 + (r_q & 1)
        return jnp.where(r_q < 2, first, second)

    fwd_to = row_slot(out_d, out_e)
    bwd_from = row_slot(in_d, in_e)
    other = c_c ^ my_c
    fwd_from = (((my_z - c_z) & 3) * 2 + other) * 4 + c_q
    bwd_to = (other * 4 + ((c_z - my_z) & 3)) * 4 + c_q

    sent = pack(features, loader_perm)
    got = lax.all_to_all(sent, ("row", "col"), split_axis=0, concat_axis=0, tiled=True)
    vals = block_values.reshape(SLOTS, BS * BS)
    own = place(got)
    fwd_blocks = prepare(vals, count, False)
    panel = [own] + alternate(lambda f: lax.ppermute(own, "col", col_hop(f, 0)), None)[0]
    sources = []
    for part in panel:
        sources += [part, lax.ppermute(part, "col", col_hop(0, 1))]

    half = list(aggregate(
        fwd_blocks, sources, fwd_from, fwd_to, count, 8, ROWS * NODE)
    )
    got_a, got_b = alternate(
        lambda d: lax.ppermute(half[d], "row", row_hop(0, d)),
        lambda e: lax.ppermute(half[4 + e], "row", row_hop(e, 0)),
    )
    n = NODE // 2
    back_count, half[0] = lax.optimization_barrier((count, half[0]))
    bwd_blocks = prepare(vals, back_count, True)
    got_a[0], bwd_blocks = lax.optimization_barrier((got_a[0], bwd_blocks))

    def partial(own_part, got, k):
        cut = slice(k * n, (k + 1) * n)
        return own_part[cut] + got[0][cut] + got[1][cut] + got[2][cut]

    sum_a = [partial(half[0], got_a, k) for k in range(SIDE)]
    sum_b = [partial(half[4], got_b, k) for k in range(SIDE)]
    rest_a = alternate(lambda e: lax.ppermute(sum_a[e], "row", row_hop(e, 0)), None)[0]
    rest_b = alternate(lambda d: lax.ppermute(sum_b[d], "row", row_hop(0, d)), None)[0]
    parts = [sum_a[0]] + rest_a + [sum_b[0]] + rest_b

    output, grad_a, grad_b, sums, gives = middle(
        parts, weight, bias_vector, cotangent, where
    )

    near_a, near_b = alternate(
        lambda e: lax.ppermute(grad_a, "row", row_hop(e, 0)),
        lambda d: lax.ppermute(grad_b, "row", row_hop(0, d)),
    )
    near_a = jnp.concatenate([grad_a] + near_a, axis=0)
    near_b = jnp.concatenate([grad_b] + near_b, axis=0)
    got_w = lax.ppermute(gives, "col", col_hop(0, 1))
    near_a, near_b, got_w = lax.optimization_barrier((near_a, near_b, got_w))
    far_a, far_b = alternate(
        lambda d: lax.ppermute(near_a, "row", row_hop(0, d)),
        lambda e: lax.ppermute(near_b, "row", row_hop(e, 0)),
    )
    column = [near_a] + far_a + [near_b] + far_b

    sums = sums + got_w
    sums = sums.reshape(SIDE, W_ROWS, F)
    got_w = [lax.ppermute(sums[f], "col", col_hop(f, 0)) for f in (1, 2, 3)]
    sums = sums[0] + got_w[0] + got_w[1] + got_w[2]
    got_w = [lax.ppermute(sums, "row", row_hop(0, d)) for d in (1, 3, 2)]
    sums = (sums + got_w[2]) + (got_w[0] + got_w[1])
    bwd_from, sums = lax.optimization_barrier((bwd_from, sums))
    got_w = lax.ppermute(sums, "col", col_hop(0, 1))
    sums = jnp.concatenate([sums, got_w], axis=0)
    keep, give = aggregate(bwd_blocks, column, bwd_from, bwd_to, count, 2, COLS * NODE)
    taken = lax.ppermute(give, "col", col_hop(0, 1))
    got_w = [lax.ppermute(sums, "row", row_hop(e, 0)) for e in (1, 3, 2)]
    sums = (sums + got_w[2]) + (got_w[0] + got_w[1])
    sums_x = [
        keep[k * NODE : (k + 1) * NODE] + taken[k * NODE : (k + 1) * NODE] for k in range(SIDE)
    ]
    got_x, _ = alternate(lambda f: lax.ppermute(sums_x[f], "col", col_hop(f, 0)), None)
    got_w = [lax.ppermute(sums, "col", col_hop(f, 0)) for f in (1, 2, 3)]
    grad_x, grad_w, grad_bias = finish(sums_x[:1] + got_x, [sums] + got_w, where)
    return (output, grad_x, grad_w, grad_bias.reshape(F))


def solution(mesh):
    in_specs = (
        P(("row", "col"), None),
        P(("row", "col")),
        P("row", "col", None, None),
        P("row", "col", None),
        P("row", "col", None),
        P("row", "col"),
        P(),
        P(),
        P(("row", "col"), None),
    )
    out_specs = (P(("row", "col"), None), P(("row", "col"), None), P(), P())

    return jax.shard_map(
        on_device, mesh=mesh, in_specs=in_specs, out_specs=out_specs, check_vma=False
    )
```

```python
import functools
import math

import jax
import jax.numpy as jnp
from jax import lax
from jax.experimental import pallas as pl
from jax.experimental.pallas import tpu as pltpu
from jax.sharding import PartitionSpec as P

F = 256
BS = 64
NODE = 256
SLOTS = 256
STEP = 64
LEAST = 32
DEPTH = 192
ROWS = 16
COLS = 8
SIDE = 4
LANES = 128
W_ROWS = 40


f32 = jnp.float32
bf16 = jnp.bfloat16


def room(mib):
    return pltpu.CompilerParams(vmem_limit_bytes=mib << 20)


def whole():
    return pl.BlockSpec(memory_space=pltpu.VMEM)


def anywhere():
    return pl.BlockSpec(memory_space=pl.ANY)


def row_hop(dy, dx):
    return [
        (y * SIDE + x, (y + dy) % SIDE * SIDE + (x + dx) % SIDE)
        for y in range(SIDE)
        for x in range(SIDE)
    ]


def row_flip(bit):
    return [(y * SIDE + x, (y ^ bit) * SIDE + x) for y in range(SIDE) for x in range(SIDE)]


def alternate(first, second):
    got = ([None] * 3, [None] * 3)
    for hop in (2, 1, 3):
        for side, send in enumerate((first, second)):
            if send is not None:
                got[side][hop - 1] = send(hop)
    return got


def col_hop(dz, dc):
    return [
        (z * 2 + c, (z + dz) % SIDE * 2 + (c + dc) % 2) for z in range(SIDE) for c in range(2)
    ]


def pick(chosen, rows):
    chosen = chosen.astype(bf16)
    high = rows.astype(bf16)
    rest = rows - high.astype(f32)
    middle_part = rest.astype(bf16)
    low = (rest - middle_part.astype(f32)).astype(bf16)
    first, second, third = (
        jnp.dot(chosen, piece, preferred_element_type=f32) for piece in (high, middle_part, low)
    )
    return (first + second) + third


def pack_kernel(features, perm_row, sent):
    owner_row = jnp.broadcast_to(lax.shift_right_logical(perm_row[...], 8), (NODE, NODE))
    owner_col = owner_row.astype(f32).T.astype(jnp.int32)
    first = lax.broadcasted_iota(jnp.int32, (NODE, NODE), 0)
    second = lax.broadcasted_iota(jnp.int32, (NODE, NODE), 1)
    earlier = (owner_col == owner_row) & (first < second)
    rank = jnp.sum(earlier.astype(f32), axis=0, keepdims=True).astype(jnp.int32)
    slot = owner_row[:1] * 2 + rank
    spot = (perm_row[...] & (NODE - 1)).astype(f32)
    rows = lax.broadcasted_iota(jnp.int32, (NODE // 2, NODE), 0)
    for n in range(2):
        chosen = (rows * 2 + n == slot).astype(f32)
        sent[:, n, :F] = pick(chosen, features[...])
        spots = jnp.sum(chosen * spot, axis=1, keepdims=True)
        sent[:, n, F:] = jnp.broadcast_to(spots, (NODE // 2, LANES))


def pack(features, perm):
    return pl.pallas_call(
        pack_kernel,
        out_shape=jax.ShapeDtypeStruct((NODE // 2, 2, F + LANES), f32),
        in_specs=[whole()] * 2,
        out_specs=whole(),
        compiler_params=room(8),
        name="pack",
    )(
        pltpu.with_memory_space_constraint(features, pltpu.HBM),
        pltpu.with_memory_space_constraint(perm.reshape(1, NODE), pltpu.HBM),
    )


def place_kernel(got, own):
    second = lax.broadcasted_iota(jnp.int32, (NODE // 2, NODE), 1)
    chosen, rows = [], []
    for n in range(2):
        spot = got[:, n, F:].astype(jnp.int32)
        chosen.append((jnp.concatenate([spot, spot], axis=1) == second).astype(f32))
        rows.append(got[:, n, :F])
    chosen = jnp.concatenate(chosen, axis=0).T
    rows = jnp.concatenate(rows, axis=0)
    own[...] = pick(chosen, rows)


def place(got):
    return pl.pallas_call(
        place_kernel,
        out_shape=jax.ShapeDtypeStruct((NODE, F), f32),
        in_specs=[whole()],
        out_specs=whole(),
        compiler_params=room(8),
        name="place",
    )(got)


def prepare_kernel(flip, count, vals, blocks, lines):
    @pl.when(pl.program_id(0) * STEP < count[0])
    def _():
        for group in range(STEP // 8):
            for tile in range(0, BS * BS // LANES, 8):
                square = jnp.stack(
                    [
                        vals[pl.ds(group * 8, 8), pl.ds((tile + t) * LANES, LANES)]
                        for t in range(8)
                    ]
                )
                square = jnp.transpose(square, (1, 0, 2))
                for slot in range(8):
                    lines[pl.ds((group * 8 + slot) * 32 + tile, 8), :] = square[slot]
        left = lax.broadcasted_iota(jnp.int32, (32, LANES), 1) < BS

        def one(slot, carry):
            pair = lines[pl.ds(pl.multiple_of(slot * 32, 32), 32), :]
            turned = pltpu.roll(pair, BS, 1)
            block = jnp.concatenate(
                [jnp.where(left, pair, turned), jnp.where(left, turned, pair)], axis=0
            )
            if flip:
                block = jnp.concatenate([block, block], axis=0).T[:BS]
            high = block.astype(bf16)
            blocks[slot, :, :LANES] = high
            blocks[slot, :, LANES:] = (block - high.astype(f32)).astype(bf16)
            return carry

        lax.fori_loop(0, STEP, one, 0, unroll=8)


def prepare(vals, count, flip):
    def at(step, count):
        return jnp.minimum(step, jnp.maximum(count[0] // STEP, 1) - 1)

    return pl.pallas_call(
        functools.partial(prepare_kernel, flip),
        out_shape=pltpu.HBM((SLOTS, BS, F), bf16),
        grid_spec=pltpu.PrefetchScalarGridSpec(
            num_scalar_prefetch=1,
            grid=(SLOTS // STEP,),
            in_specs=[pl.BlockSpec((STEP, BS * BS), lambda s, n: (at(s, n), 0))],
            out_specs=pl.BlockSpec((STEP, BS, F), lambda s, n: (at(s, n), 0, 0)),
            scratch_shapes=[pltpu.VMEM((STEP * 32, LANES), f32)],
        ),
        cost_estimate=pl.CostEstimate(flops=10**8, bytes_accessed=12 << 20, transcendentals=0),
        compiler_params=room(12),
        name="prepare_back" if flip else "prepare",
    )(count, pltpu.with_memory_space_constraint(vals, pltpu.HBM))


def aggregate_kernel(n_src, n_dst, source_at, target_at, count, blocks, *refs):
    sources, targets = refs[:n_src], refs[n_src : n_src + n_dst]
    held, split, total, stage, in_sems, out_sems, block_sems = refs[n_src + n_dst :]
    in_rows = sources[0].shape[0]
    out_rows = targets[0].shape[0]
    full = count[0] // STEP

    def fetch(step, slot):
        return pltpu.make_async_copy(
            blocks.at[pl.ds(step * STEP, STEP)], stage.at[slot], block_sems.at[slot]
        )

    def load(n):
        return pltpu.make_async_copy(
            sources[n], held.at[pl.ds(n * in_rows, in_rows)], in_sems.at[n]
        )

    def keep(n):
        return pltpu.make_async_copy(
            total.at[pl.ds(n * out_rows, out_rows)], targets[n], out_sems.at[n]
        )

    for n in range(n_src):
        load(n).start()
    fetch(0, 0).start()
    total[...] = jnp.zeros_like(total)
    per = in_rows // BS
    for n in range(n_src):
        load(n).wait()

        def one_block(k, carry):
            at = n * per + k
            rows = held[pl.ds(pl.multiple_of(at * BS, BS), BS), :]
            high = rows.astype(bf16)
            low = (rows - high.astype(f32)).astype(bf16)
            split[at, 0:BS, :] = high
            split[at, BS : 2 * BS, :] = low
            split[at, 2 * BS :, :] = high
            return carry

        lax.fori_loop(0, per, one_block, 0, unroll=2)

    def slots(step, place, number):
        for slot in range(number):
            at = step * STEP + slot
            term = jnp.dot(
                stage[place, slot][:, :DEPTH], split[source_at[at]], preferred_element_type=f32
            )
            into = pl.ds(pl.multiple_of(target_at[at] * BS, BS), BS)
            total[into, :] += term

    def one_step(step, carry):
        place = step & 1
        fetch(step, place).wait()

        @pl.when(step + 1 < full)
        def _():
            fetch(step + 1, 1 - place).start()

        slots(step, place, STEP)
        return carry

    lax.fori_loop(0, full, one_step, 0)

    @pl.when(count[0] == LEAST)
    def _():
        fetch(0, 0).wait()
        slots(0, 0, LEAST)

    for n in range(n_dst):
        keep(n).start()
    for n in range(n_dst):
        keep(n).wait()


def aggregate(blocks, sources, source_at, target_at, count, n_dst, out_rows):
    n_src = len(sources)
    total_in = sum(s.shape[0] for s in sources)
    return pl.pallas_call(
        functools.partial(aggregate_kernel, n_src, n_dst),
        out_shape=[jax.ShapeDtypeStruct((out_rows // n_dst, F), f32)] * n_dst,
        in_specs=[pl.BlockSpec(memory_space=pltpu.SMEM)] * 3 + [anywhere()] * (n_src + 1),
        out_specs=[anywhere()] * n_dst,
        scratch_shapes=[
            pltpu.VMEM((total_in, F), f32),
            pltpu.VMEM((total_in // BS, DEPTH, F), bf16),
            pltpu.VMEM((out_rows, F), f32),
            pltpu.VMEM((2, STEP, BS, F), bf16),
            pltpu.SemaphoreType.DMA((n_src,)),
            pltpu.SemaphoreType.DMA((n_dst,)),
            pltpu.SemaphoreType.DMA((2,)),
        ],
        cost_estimate=pl.CostEstimate(
            flops=2 * SLOTS * BS * F * F, bytes_accessed=16 << 20, transcendentals=0
        ),
        compiler_params=room(18),
    )(
        source_at,
        target_at,
        count,
        pltpu.with_memory_space_constraint(blocks, pltpu.HBM),
        *sources,
    )


def halves(rows):
    high = rows.astype(bf16)
    return high, (rows - high.astype(f32)).astype(bf16)


def product(left, right, dims):
    (a, b), (c, d) = halves(left), halves(right)

    def dot(u, v):
        return lax.dot_general(u, v, (dims, ((), ())), preferred_element_type=f32)

    return dot(a, c) + (dot(a, d) + dot(b, c))


def middle_kernel(*refs):
    where, parts, (weight, bias, cotangent) = refs[0], refs[1:9], refs[9:12]
    output, grad_a, grad_b, sums, gives, hidden, turned, strip = refs[12:]
    half = NODE // 2
    hidden[:half] = parts[0][...] + parts[1][...] + parts[2][...] + parts[3][...]
    hidden[half:] = parts[4][...] + parts[5][...] + parts[6][...] + parts[7][...]
    for side in range(2):
        lanes = slice(side * LANES, (side + 1) * LANES)
        strip[side * NODE : (side + 1) * NODE] = cotangent[:, lanes]
        for q in range(NODE // BS):
            for odd in range(2):
                turned[pl.ds(q * BS + odd * 32, 32), lanes] = strip[
                    pl.ds(side * NODE + q * BS + odd, 32, stride=2), :
                ]
    rows = hidden[...]
    preact = product(rows, weight[...], ((1,), (0,)))
    preact = preact + bias[...]
    squashed = 1.0 / (1.0 + jnp.exp(-preact))
    grad_pre = turned[...] * squashed * (1.0 + preact * (1.0 - squashed))
    turned[...] = preact * squashed
    grad = product(grad_pre, weight[...], ((1,), (1,)))
    grad_a[...] = grad[:half]
    grad_b[...] = grad[half:]
    for side in range(2):
        lanes = slice(side * LANES, (side + 1) * LANES)
        for q in range(NODE // BS):
            for odd in range(2):
                strip[pl.ds(side * NODE + q * BS + odd, 32, stride=2), :] = turned[
                    pl.ds(q * BS + odd * 32, 32), lanes
                ]
        output[:, lanes] = strip[side * NODE : (side + 1) * NODE]
    turned[...] = product(rows.T, grad_pre, ((1,), (0,)))
    local_b = jnp.sum(grad_pre, axis=0, keepdims=True)
    for f in range(SIDE):
        ahead = ((where[0] + f) & 3) * 2
        for side, into in ((where[1], sums), (1 - where[1], gives)):
            at = pl.multiple_of((ahead + side) * 32, 32)
            into[f * W_ROWS : f * W_ROWS + 32, :] = turned[pl.ds(at, 32), :]
            into[f * W_ROWS + 32 : (f + 1) * W_ROWS, :] = jnp.broadcast_to(
                local_b, (W_ROWS - 32, F)
            )


def middle(parts, weight, bias, cotangent, where):
    return pl.pallas_call(
        middle_kernel,
        out_shape=[
            jax.ShapeDtypeStruct((NODE, F), f32),
            jax.ShapeDtypeStruct((NODE // 2, F), f32),
            jax.ShapeDtypeStruct((NODE // 2, F), f32),
            jax.ShapeDtypeStruct((SIDE * W_ROWS, F), f32),
            jax.ShapeDtypeStruct((SIDE * W_ROWS, F), f32),
        ],
        in_specs=[pl.BlockSpec(memory_space=pltpu.SMEM)] + [whole()] * 11,
        out_specs=[whole()] * 5,
        scratch_shapes=[pltpu.VMEM((NODE, F), f32)] * 2 + [pltpu.VMEM((2 * NODE, LANES), f32)],
        compiler_params=room(12),
        name="middle",
    )(where, *parts, weight, bias.reshape(1, F), cotangent)


def finish_kernel(where, *refs):
    pieces, sums, (grad_x, grad_w, grad_b) = refs[:4], refs[4:8], refs[8:]
    grad_x[...] = pieces[0][...] + pieces[1][...] + pieces[2][...] + pieces[3][...]
    scale = 1.0 / math.sqrt(NODE * ROWS * COLS)
    for f in range(SIDE):
        chip = ((where[0] - f) & 3) * 2
        for side in range(2):
            n = chip + (where[1] ^ side)
            rows = sums[f][side * W_ROWS : (side + 1) * W_ROWS, :] * scale
            grad_w[pl.ds(pl.multiple_of(n * 32, 32), 32), :] = rows[:32]

            @pl.when(n == 0)
            def _():
                grad_b[...] = rows[32:33]


def finish(pieces, sums, where):
    return pl.pallas_call(
        finish_kernel,
        out_shape=[
            jax.ShapeDtypeStruct((NODE, F), f32),
            jax.ShapeDtypeStruct((F, F), f32),
            jax.ShapeDtypeStruct((1, F), f32),
        ],
        in_specs=[pl.BlockSpec(memory_space=pltpu.SMEM)] + [whole()] * 8,
        out_specs=[whole()] * 3,
        compiler_params=room(8),
        name="finish",
    )(where, *pieces, *sums)


def on_device(
    features,
    loader_perm,
    block_values,
    block_row,
    block_column,
    tile_count,
    weight,
    bias_vector,
    cotangent,
):
    row = lax.axis_index("row")
    col = lax.axis_index("col")
    my_y, my_x = row // SIDE, row % SIDE
    my_z, my_c = col // 2, col % 2
    where = jnp.stack([my_z, my_c])
    count = tile_count.reshape(1)
    tile_rows = block_row.reshape(SLOTS)
    tile_columns = block_column.reshape(SLOTS)

    r_dev, r_q = tile_rows >> 2, tile_rows & 3
    r_y, r_x = r_dev >> 2, r_dev & 3
    c_dev, c_q = tile_columns >> 2, tile_columns & 3
    c_z, c_c = c_dev >> 1, c_dev & 1
    out_d, out_e = (r_x - my_x) & 3, (r_y - my_y) & 3
    in_d, in_e = (my_x - r_x) & 3, (my_y - r_y) & 3

    def row_slot(d, e):
        first = d * 8 + e * 2 + (r_q & 1)
        second = 32 + e * 8 + d * 2 + (r_q & 1)
        return jnp.where(r_q < 2, first, second)

    fwd_to = row_slot(out_d, out_e)
    bwd_from = row_slot(in_d, in_e)
    other = c_c ^ my_c
    fwd_from = (((my_z - c_z) & 3) * 2 + other) * 4 + c_q
    bwd_to = (other * 4 + ((c_z - my_z) & 3)) * 4 + c_q

    sent = pack(features, loader_perm)
    got = lax.all_to_all(sent, ("row", "col"), split_axis=0, concat_axis=0, tiled=True)
    vals = block_values.reshape(SLOTS, BS * BS)
    own = place(got)
    fwd_blocks = prepare(vals, count, False)
    panel = [own] + alternate(lambda f: lax.ppermute(own, "col", col_hop(f, 0)), None)[0]
    sources = []
    for part in panel:
        sources += [part, lax.ppermute(part, "col", col_hop(0, 1))]

    half = list(aggregate(
        fwd_blocks, sources, fwd_from, fwd_to, count, 8, ROWS * NODE)
    )
    got_a, got_b = alternate(
        lambda d: lax.ppermute(half[d], "row", row_hop(0, d)),
        lambda e: lax.ppermute(half[4 + e], "row", row_hop(e, 0)),
    )
    n = NODE // 2
    back_count, half[0] = lax.optimization_barrier((count, half[0]))
    bwd_blocks = prepare(vals, back_count, True)
    got_a[0], bwd_blocks = lax.optimization_barrier((got_a[0], bwd_blocks))

    def partial(own_part, got, k):
        cut = slice(k * n, (k + 1) * n)
        return own_part[cut] + got[0][cut] + got[1][cut] + got[2][cut]

    sum_a = [partial(half[0], got_a, k) for k in range(SIDE)]
    sum_b = [partial(half[4], got_b, k) for k in range(SIDE)]
    rest_a = alternate(lambda e: lax.ppermute(sum_a[e], "row", row_hop(e, 0)), None)[0]
    rest_b = alternate(lambda d: lax.ppermute(sum_b[d], "row", row_hop(0, d)), None)[0]
    parts = [sum_a[0]] + rest_a + [sum_b[0]] + rest_b

    output, grad_a, grad_b, sums, gives = middle(
        parts, weight, bias_vector, cotangent, where
    )

    near_a, near_b = alternate(
        lambda e: lax.ppermute(grad_a, "row", row_hop(e, 0)),
        lambda d: lax.ppermute(grad_b, "row", row_hop(0, d)),
    )
    near_a = jnp.concatenate([grad_a] + near_a, axis=0)
    near_b = jnp.concatenate([grad_b] + near_b, axis=0)
    got_w = lax.ppermute(gives, "col", col_hop(0, 1))
    near_a, near_b, got_w = lax.optimization_barrier((near_a, near_b, got_w))
    far_a, far_b = alternate(
        lambda d: lax.ppermute(near_a, "row", row_hop(0, d)),
        lambda e: lax.ppermute(near_b, "row", row_hop(e, 0)),
    )
    column = [near_a] + far_a + [near_b] + far_b

    sums = sums + got_w
    sums = sums.reshape(SIDE, W_ROWS, F)
    got_w = [lax.ppermute(sums[f], "col", col_hop(f, 0)) for f in (1, 2, 3)]
    sums = sums[0] + got_w[0] + got_w[1] + got_w[2]
    got_w = [lax.ppermute(sums, "row", row_hop(0, d)) for d in (1, 3, 2)]
    sums = (sums + got_w[2]) + (got_w[0] + got_w[1])
    bwd_from, sums = lax.optimization_barrier((bwd_from, sums))
    sums = sums + lax.ppermute(sums, "row", row_flip(1))
    keep, give = aggregate(bwd_blocks, column, bwd_from, bwd_to, count, 2, COLS * NODE)
    taken = lax.ppermute(give, "col", col_hop(0, 1))
    sums = sums + lax.ppermute(sums, "row", row_flip(2))
    sums_x = [
        keep[k * NODE : (k + 1) * NODE] + taken[k * NODE : (k + 1) * NODE] for k in range(SIDE)
    ]
    got_x, _ = alternate(lambda f: lax.ppermute(sums_x[f], "col", col_hop(f, 0)), None)
    got_w = lax.ppermute(sums, "col", col_hop(0, 1))
    sums = jnp.concatenate([sums, got_w], axis=0)
    got_w = [lax.ppermute(sums, "col", col_hop(f, 0)) for f in (1, 2, 3)]
    grad_x, grad_w, grad_bias = finish(sums_x[:1] + got_x, [sums] + got_w, where)
    return (output, grad_x, grad_w, grad_bias.reshape(F))


def solution(mesh):
    in_specs = (
        P(("row", "col"), None),
        P(("row", "col")),
        P("row", "col", None, None),
        P("row", "col", None),
        P("row", "col", None),
        P("row", "col"),
        P(),
        P(),
        P(("row", "col"), None),
    )
    out_specs = (P(("row", "col"), None), P(("row", "col"), None), P(), P())

    return jax.shard_map(
        on_device, mesh=mesh, in_specs=in_specs, out_specs=out_specs, check_vma=False
    )
```
